256 devices in a mesh: sym: 8 (over y, core), rows: 32 (over z, x).
Axes of the slice: x: 4, y: 4, z: 8, core: 2. Of those that a mesh axis runs over, the one named last changes fastest.
Arguments:
- coeffs: bfloat16 [16384, 8192], P('rows', 'sym'), may hold values from -6 to 6
- beta_op: bfloat16 [8, 1024, 1024], P('sym'), may hold values from -0.1875 to 0.1875
- mix_op: bfloat16 [8, 8, 8, 128, 128], P('sym'), may hold values from -0.125 to 0.125
- pair_op: bfloat16 [8, 128, 128], replicated, may hold values from -0.1875 to 0.1875
- send_list: int32 [32, 32, 2], replicated, may hold values from -1 to 3, as said below
- mix_slot: int32 [128, 16], replicated, may hold values from 0 to 63, as said below
- mix_sign: int32 [128, 16], replicated, may hold values from 0 to 1
- mix_pair: int32 [128, 16], replicated, may hold values from 0 to 7
- aa_src: int32 [128, 8], replicated, may hold values from 0 to 127
- aa_sign: int32 [128, 8], replicated, may hold values from 0 to 1
- aa_pair: int32 [128, 8], replicated, may hold values from 0 to 7
Outputs:
- sigma: float32 [16384, 8192], P('rows', 'sym')
The draws below stay inside these ranges and needn't reach their ends.
Inputs may be any that keep to these rules, and one draw needn't show every extreme that they name: send_list[s, r, c] is the block, counted within device s's own 4 alpha blocks, that s sends to device r in slot c, or -1 for an empty slot; live slots of a pair come first and hold distinct blocks; every device sends at least one block to itself; in every draw some device receives 2 blocks from every device. mix_slot[P, l] = s * 2 + c names slot c of send_list[s, P // 4], always a live one; every live slot sent to a device is named by some entry of that device's destination blocks.
All inputs are finite; a program needn't handle non-finite values.
Results may differ from the reference program's by a relative error of at most 0.0075.
Values may be sent and summed in bfloat16 or wider, within the bound.
No kernel may reach another device: no remote copies, remote signals or barrier semaphores. Data moves between devices by JAX's collectives and lax.ppermute only.
A program may use at most 128 MiB of HBM per device.

```python
import jax
import jax.numpy as jnp
from jax import lax

TILE = 128
BT = 8
ABLK = 4
CAP = 2
ENTRIES = 16
KA = 8
NPA = 8
RANKS = 32
SECTORS = 8
NBLK = 128
NA = 16384
BS = 1024
NB = 8192


def routing(key):
    base = jax.random.fold_in(key, 4021)
    key_list = jax.random.split(base, 6)
    full_dest = jax.random.randint(key_list[0], (), 0, RANKS)
    src_ids = jnp.arange(RANKS)[:, None]
    dst_ids = jnp.arange(RANKS)[None, :]
    counts = jax.random.randint(key_list[1], (RANKS, RANKS), 0, CAP + 1)
    counts = jnp.where(dst_ids == full_dest, CAP, counts)
    counts = jnp.where(src_ids == dst_ids, jnp.maximum(counts, 1), counts)
    scores = jax.random.randint(key_list[2], (RANKS, RANKS, ABLK), 0, 1 << 20) * ABLK + jnp.arange(ABLK)
    block_order = jnp.argsort(scores, axis=-1, stable=True)[:, :, :CAP]
    slot_ids = jnp.arange(CAP)
    live_slot = slot_ids[None, None, :] < counts[:, :, None]
    sends = jnp.where(live_slot, block_order, -1).astype(jnp.int32)
    slot_total = RANKS * CAP
    live_dest = jnp.transpose(live_slot, (1, 0, 2)).reshape(RANKS, slot_total)
    jitter = jax.random.randint(key_list[3], (RANKS, slot_total), 0, 1 << 20) * slot_total + jnp.arange(slot_total)
    ranked = jnp.argsort(jnp.where(live_dest, -jitter - 1, jitter), axis=-1, stable=True)
    live_count = jnp.sum(live_dest.astype(jnp.int32), axis=-1)
    entry_total = ABLK * ENTRIES
    entry_ids = jnp.arange(entry_total)[None, :]
    picked = jax.random.randint(key_list[4], (RANKS, entry_total), 0, 1 << 20) % live_count[:, None]
    positions = jnp.where(entry_ids < live_count[:, None], entry_ids, picked)
    chosen = jnp.take_along_axis(ranked, positions, axis=1)
    shuffle = jnp.argsort(jax.random.randint(key_list[5], (RANKS, entry_total), 0, 1 << 20) * entry_total + entry_ids, axis=-1, stable=True)
    chosen = jnp.take_along_axis(chosen, shuffle, axis=1)
    return (sends, chosen.reshape(RANKS * ABLK, ENTRIES).astype(jnp.int32))


def draw_send_list(key, part):
    return routing(key)[0]


def draw_mix_slot(key, part):
    return routing(key)[1]


def place_ends(result, stream_key, low, high):
    index_at = [jax.random.randint(jax.random.fold_in(stream_key, axis), (), 0, length) for axis, length in enumerate(result.shape)]
    longest = result.shape.index(max(result.shape))
    neighbour = index_at[:longest] + [(index_at[longest] + 1) % result.shape[longest]] + index_at[longest + 1:]
    return result.at[tuple(index_at)].set(low).at[tuple(neighbour)].set(high)


def level_of(stream_key, extent, shards, low, top_value):
    def one(dim, parts):
        steps = jax.random.uniform(jax.random.fold_in(jax.random.fold_in(stream_key, 6), dim), (parts,), jnp.float32, low / len(shards), top_value / len(shards))
        return jnp.repeat(jnp.exp(steps), extent[dim] // parts).reshape((-1,) + (1,) * (len(extent) - dim - 1))

    gain = one(*shards[0])
    for cut in shards[1:]:
        gain = gain * one(*cut)
    return gain


def scatter_about(own_key, shape, deviation, most, cuts=(), kind=jnp.bfloat16):
    level = level_of(own_key, shape, cuts, -0.22, 0.18) if cuts else 1.0
    values = jax.random.normal(own_key, shape, jnp.float32) * deviation * level
    return jnp.minimum(jnp.maximum(values, -most), most).astype(kind)


def setup_inputs(seed: int = 0) -> dict:
    seeds = jax.random.split(jax.random.key(seed), 12)
    coeffs = scatter_about(seeds[0], (NA, NB), 1.0, 6.0, ((0, 32), (1, 8)))
    beta_op = scatter_about(seeds[1], (SECTORS, BS, BS), BS ** -0.5, 0.1875, ((0, 8),))
    mix_op = scatter_about(seeds[2], (SECTORS, SECTORS, BT, TILE, TILE), (TILE * ENTRIES) ** -0.5, 0.125, ((0, 8),))
    pair_op = scatter_about(seeds[3], (NPA, TILE, TILE), (TILE * KA) ** -0.5, 0.1875)
    send_list = draw_send_list(jax.random.fold_in(seeds[11], 71), 0)
    mix_slot = draw_mix_slot(jax.random.fold_in(seeds[11], 71), 0)
    mix_sign = place_ends(jax.random.randint(seeds[6], (NBLK, ENTRIES), 0, 2), jax.random.fold_in(seeds[6], 1), 0, 1).astype(jnp.int32)
    mix_pair = place_ends(jax.random.randint(seeds[7], (NBLK, ENTRIES), 0, SECTORS), jax.random.fold_in(seeds[7], 1), 0, SECTORS - 1).astype(jnp.int32)
    aa_src = place_ends(jax.random.randint(seeds[8], (NBLK, KA), 0, NBLK), jax.random.fold_in(seeds[8], 1), 0, NBLK - 1).astype(jnp.int32)
    aa_sign = place_ends(jax.random.randint(seeds[9], (NBLK, KA), 0, 2), jax.random.fold_in(seeds[9], 1), 0, 1).astype(jnp.int32)
    aa_pair = place_ends(jax.random.randint(seeds[10], (NBLK, KA), 0, NPA), jax.random.fold_in(seeds[10], 1), 0, NPA - 1).astype(jnp.int32)
    return {"coeffs": coeffs, "beta_op": beta_op, "mix_op": mix_op, "pair_op": pair_op, "send_list": send_list, "mix_slot": mix_slot, "mix_sign": mix_sign, "mix_pair": mix_pair, "aa_src": aa_src, "aa_sign": aa_sign, "aa_pair": aa_pair}


def reround(values):
    narrow = lax.optimization_barrier(values.astype(jnp.bfloat16))
    return narrow.astype(jnp.float32)


def reference(coeffs, beta_op, mix_op, pair_op, send_list, mix_slot, mix_sign, mix_pair, aa_src, aa_sign, aa_pair):
    blocks = coeffs.reshape(NBLK, TILE, NB)
    pieces = []
    for sector in range(SECTORS):
        pieces.append(jnp.dot(coeffs[:, sector * BS:(sector + 1) * BS], beta_op[sector], preferred_element_type=jnp.float32))
    beta_part = jnp.concatenate(pieces, axis=1)

    slot_src = (mix_slot // CAP).astype(jnp.int32)
    slot_pos = (mix_slot % CAP).astype(jnp.int32)
    dest_rank = (jnp.arange(NBLK, dtype=jnp.int32) // ABLK)[:, None]
    source = slot_src * ABLK + send_list[slot_src, dest_rank, slot_pos]
    mixed_sign = (1 - 2 * mix_sign).astype(jnp.float32)
    pair_ids = jnp.arange(SECTORS, dtype=jnp.int32)
    flipped = jnp.bitwise_xor(pair_ids[:, None], pair_ids[None, :])
    chosen_ops = mix_op[flipped, pair_ids[None, :]].astype(jnp.float32)

    def mixed_block(inputs):
        src_row, sign_row, pair_row = inputs
        picked = blocks[src_row].astype(jnp.float32)
        weights = sign_row[None, :] * (pair_row[None, :] == pair_ids[:, None]).astype(jnp.float32)
        combo = reround(jnp.einsum('gl,lin->gin', weights, picked))
        combo = combo.reshape(SECTORS, TILE, SECTORS, BT, TILE)
        selected = combo[pair_ids[None, :], :, flipped]
        terms = reround(jnp.einsum('dgitk,dgtkj->dgitj', selected, chosen_ops))
        summed = jnp.sum(terms, axis=1)
        return jnp.transpose(summed, (1, 0, 2, 3)).reshape(TILE, NB)

    mixed_part = lax.map(mixed_block, (source, mixed_sign, mix_pair)).reshape(NA, NB)

    alpha_sign = (1 - 2 * aa_sign).astype(jnp.float32)
    operator_ids = jnp.arange(NPA, dtype=jnp.int32)
    pair_float = pair_op.astype(jnp.float32)

    def alpha_block(inputs):
        src_row, sign_row, pair_row = inputs
        picked = blocks[src_row].astype(jnp.float32)
        weights = sign_row[None, :] * (pair_row[None, :] == operator_ids[:, None]).astype(jnp.float32)
        combo = reround(jnp.einsum('gk,kin->gin', weights, picked))
        return jnp.einsum('gij,gjn->in', pair_float, combo)

    alpha_part = lax.map(alpha_block, (aa_src, alpha_sign, aa_pair)).reshape(NA, NB)
    return beta_part + alpha_part + mixed_part
```

```python
import jax
import jax.numpy as jnp
from jax import lax
from jax.experimental import pallas as pl
from jax.experimental.pallas import tpu as pltpu
from jax.sharding import PartitionSpec as P

TILE = 128
ABLK = 4
CAP = 2
OPS = 8
SECTORS = 8
RANKS = 32
XDIM = 4
TILES = 8
NBLK = 128
BF = jnp.bfloat16
F32 = jnp.float32
VMEM_BYTES = 56 * 1024 * 1024


def interleave(rows, cols):
    r = lax.broadcasted_iota(jnp.int32, (rows, cols), 0)
    k = lax.broadcasted_iota(jnp.int32, (rows, cols), 1)
    return (k == (r % ABLK) * TILE + r // ABLK).astype(F32).astype(BF)


def deinterleave(rows, cols):
    r = lax.broadcasted_iota(jnp.int32, (rows, cols), 0)
    k = lax.broadcasted_iota(jnp.int32, (rows, cols), 1)
    return (r == (k % ABLK) * TILE + k // ABLK).astype(F32).astype(BF)


def pack_kernel(c_ref, send_ref):
    order = interleave(512, 512)
    for t in range(TILES):
        cols = slice(t * TILE, (t + 1) * TILE)
        block = c_ref[:, cols]
        turned = jnp.concatenate(
            [block[p * TILE : (p + 1) * TILE].astype(F32).T.astype(BF) for p in range(ABLK)], axis=0
        )
        both = jnp.concatenate([block, turned], axis=1)
        moved = jnp.dot(order, both, preferred_element_type=F32).astype(BF)
        for kind in range(2):
            part = moved[:, kind * TILE : (kind + 1) * TILE]
            send_ref[:, t, :, kind] = part.reshape(SECTORS, XDIM, 16, TILE)


def swap_halves(first, second):
    low = lax.broadcasted_iota(jnp.int32, first.shape, 1) < 4
    lo = jnp.where(low, first, pltpu.roll(second, 4, 1))
    hi = jnp.where(low, pltpu.roll(first, 4, 1), second)
    return lo, hi


def middle_kernel(recv_ref, mix_ref, pair_ref, wm_ref, wa_ref, out_ref, x_ref, c_ref):
    for kind in range(2):
        w_ref = (wm_ref, wa_ref)[kind]

        @pl.loop(0, SECTORS)
        def _(s):
            got = recv_ref[s, :, kind].astype(F32).reshape(16, 2, 2, 8, TILE)
            for h in range(2):
                lo, hi = swap_halves(got[:, 0, h], got[:, 1, h])
                x_ref[s, 2 * h] = lo.reshape(TILE, TILE).astype(BF)
                x_ref[s, 2 * h + 1] = hi.reshape(TILE, TILE).astype(BF)

        weights = jnp.concatenate(
            [w_ref[:, g * TILE : (g + 1) * TILE] for g in range(OPS)], axis=0
        )

        @pl.loop(0, SECTORS // 2)
        def _(half):
            s = half * 2
            for a in range(ABLK):
                pair = jnp.concatenate([x_ref[s, a], x_ref[s + 1, a]], axis=1)
                combo = jnp.dot(weights, pair, preferred_element_type=F32).astype(BF)
                for g in range(OPS):
                    rows = combo[g * TILE : (g + 1) * TILE]
                    for o in range(2):
                        dest = (s + o) ^ g if kind == 0 else s + o
                        c_ref[dest, a * TILE : (a + 1) * TILE, g * TILE : (g + 1) * TILE] = rows[
                            :, o * TILE : (o + 1) * TILE
                        ]

        @pl.loop(0, SECTORS)
        def _(d):
            if kind == 0:
                ops = jnp.concatenate([mix_ref[d ^ g, g] for g in range(OPS)], axis=0)
            else:
                ops = pair_ref[...]
            res = jnp.dot(c_ref[d], ops, preferred_element_type=F32)
            sides = []
            for h in range(2):
                first = res[2 * h * TILE : (2 * h + 1) * TILE].reshape(16, 8, TILE)
                second = res[(2 * h + 1) * TILE : (2 * h + 2) * TILE].reshape(16, 8, TILE)
                sides.append(swap_halves(first, second))
            for o in range(2):
                both = jnp.concatenate([sides[0][o][:, None], sides[1][o][:, None]], axis=1)
                out_ref[d, :, o, kind] = both.reshape(16, 16, TILE).astype(BF)


def unpack_kernel(recv_ref, beta_ref, out_ref):
    order = deinterleave(512, 512)
    for t in range(TILES):
        cols = slice(t * TILE, (t + 1) * TILE)
        both = jnp.concatenate(
            [recv_ref[:, t, :, kind].reshape(512, TILE) for kind in range(2)], axis=1
        )
        moved = jnp.dot(order, both, preferred_element_type=F32)
        for p in range(ABLK):
            rows = slice(p * TILE, (p + 1) * TILE)
            out_ref[rows, cols] = beta_ref[rows, cols] + moved[rows, :TILE] + moved[rows, TILE:].T


def call(kernel, out_shape, scratch=()):
    return pl.pallas_call(
        kernel,
        out_shape=out_shape,
        scratch_shapes=list(scratch),
        compiler_params=pltpu.CompilerParams(vmem_limit_bytes=VMEM_BYTES),
    )


def signed_weights(source, sign, pair):
    key = pair * NBLK + source
    ids = jnp.arange(OPS * NBLK, dtype=jnp.int32)
    hit = key[:, :, None] == ids[None, None, :]
    factor = (1 - 2 * sign).astype(F32)
    return jnp.sum(jnp.where(hit, factor[:, :, None], 0.0), axis=1).astype(BF)


def per_device(
    coeffs,
    beta_op,
    mix_op,
    pair_op,
    send_list,
    mix_slot,
    mix_sign,
    mix_pair,
    aa_src,
    aa_sign,
    aa_pair,
):
    tile = lax.axis_index("rows") // XDIM
    mine = lax.dynamic_index_in_dim(mix_op[0], tile, axis=1, keepdims=False)
    mix_all = lax.all_gather(mine, "sym", axis=0)

    send = call(
        pack_kernel, jax.ShapeDtypeStruct((SECTORS, TILES, XDIM, 2, 16, TILE), BF)
    )(coeffs)
    recv = lax.all_to_all(
        send.reshape(256, 32, TILE), ("sym", "rows"), split_axis=0, concat_axis=0, tiled=True
    )

    table = jnp.transpose(send_list, (1, 0, 2)).reshape(RANKS, RANKS * CAP)
    slots = jnp.arange(RANKS * CAP, dtype=jnp.int32)
    table = jnp.broadcast_to(table[:, None, :], (RANKS, ABLK, RANKS * CAP)).reshape(NBLK, 1, RANKS * CAP)
    owned = jnp.sum(jnp.where(mix_slot[:, :, None] == slots[None, None, :], table, 0), axis=2)
    source = (mix_slot // CAP) * ABLK + owned
    w_mix = signed_weights(source, mix_sign, mix_pair)
    w_alpha = signed_weights(aa_src, aa_sign, aa_pair)
    pairs = jnp.transpose(pair_op, (0, 2, 1)).reshape(OPS * TILE, TILE)

    back = call(
        middle_kernel,
        jax.ShapeDtypeStruct((SECTORS, 16, 2, 2, 16, TILE), BF),
        (
            pltpu.VMEM((SECTORS, ABLK, TILE, TILE), BF),
            pltpu.VMEM((SECTORS, 4 * TILE, OPS * TILE), BF),
        ),
    )(recv.reshape(SECTORS, RANKS, 2, 16, TILE), mix_all, pairs, w_mix, w_alpha)
    home = lax.all_to_all(
        back.reshape(256, 32, TILE), ("sym", "rows"), split_axis=0, concat_axis=0, tiled=True
    )
    beta_part = jnp.dot(coeffs, beta_op[0], preferred_element_type=F32)
    return call(unpack_kernel, jax.ShapeDtypeStruct(coeffs.shape, F32))(
        home.reshape(SECTORS, TILES, XDIM, 2, 16, TILE), beta_part
    )


def solution(mesh):
    in_specs = (
        P("rows", "sym"),
        P("sym", None, None),
        P("sym", None, None, None, None),
        P(),
        P(),
        P(),
        P(),
        P(),
        P(),
        P(),
        P(),
    )
    out_specs = P("rows", "sym")
    return jax.shard_map(
        per_device, mesh=mesh, in_specs=in_specs, out_specs=out_specs, check_vma=False
    )
```

```python
import jax
import jax.numpy as jnp
from jax import lax
from jax.experimental import pallas as pl
from jax.experimental.pallas import tpu as pltpu
from jax.sharding import PartitionSpec as P

TILE = 128
ABLK = 4
CAP = 2
OPS = 8
SECTORS = 8
RANKS = 32
XDIM = 4
TILES = 8
NBLK = 128
BF = jnp.bfloat16
F32 = jnp.float32
VMEM_BYTES = 56 * 1024 * 1024


def interleave(rows, cols):
    r = lax.broadcasted_iota(jnp.int32, (rows, cols), 0)
    k = lax.broadcasted_iota(jnp.int32, (rows, cols), 1)
    return (k == (r % ABLK) * TILE + r // ABLK).astype(F32).astype(BF)


def deinterleave(rows, cols):
    r = lax.broadcasted_iota(jnp.int32, (rows, cols), 0)
    k = lax.broadcasted_iota(jnp.int32, (rows, cols), 1)
    return (r == (k % ABLK) * TILE + k // ABLK).astype(F32).astype(BF)


def pack_kernel(c_ref, send_ref):
    order = interleave(512, 512)
    for t in range(TILES):
        cols = slice(t * TILE, (t + 1) * TILE)
        block = c_ref[:, cols]
        turned = jnp.concatenate(
            [block[p * TILE : (p + 1) * TILE].astype(F32).T.astype(BF) for p in range(ABLK)], axis=0
        )
        both = jnp.concatenate([block, turned], axis=1)
        moved = jnp.dot(order, both, preferred_element_type=F32).astype(BF)
        for kind in range(2):
            part = moved[:, kind * TILE : (kind + 1) * TILE]
            send_ref[:, t, :, kind] = part.reshape(SECTORS, XDIM, 16, TILE)


def swap_halves(first, second):
    low = lax.broadcasted_iota(jnp.int32, first.shape, 1) < 4
    lo = jnp.where(low, first, pltpu.roll(second, 4, 1))
    hi = jnp.where(low, pltpu.roll(first, 4, 1), second)
    return lo, hi


def middle_kernel(
    recv_ref, same_ref, other_ref, pair_ref, wm_ref, wa_ref, out_ref, x_ref, c_ref, mix_ref
):
    sector = lax.axis_index("sym")
    for k in range(SECTORS // 2):
        mix_ref[2 * k] = same_ref[k]
        mix_ref[2 * k + 1] = other_ref[k]
    for kind in range(2):
        w_ref = (wm_ref, wa_ref)[kind]

        @pl.loop(0, SECTORS)
        def _(s):
            got = recv_ref[s, :, kind].astype(F32).reshape(16, 2, 2, 8, TILE)
            for h in range(2):
                lo, hi = swap_halves(got[:, 0, h], got[:, 1, h])
                x_ref[s, 2 * h] = lo.reshape(TILE, TILE).astype(BF)
                x_ref[s, 2 * h + 1] = hi.reshape(TILE, TILE).astype(BF)

        weights = jnp.concatenate(
            [w_ref[:, g * TILE : (g + 1) * TILE] for g in range(OPS)], axis=0
        )

        @pl.loop(0, SECTORS // 2)
        def _(half):
            s = half * 2
            for a in range(ABLK):
                pair = jnp.concatenate([x_ref[s, a], x_ref[s + 1, a]], axis=1)
                combo = jnp.dot(weights, pair, preferred_element_type=F32).astype(BF)
                for g in range(OPS):
                    rows = combo[g * TILE : (g + 1) * TILE]
                    for o in range(2):
                        dest = (s + o) ^ g if kind == 0 else s + o
                        c_ref[dest, a * TILE : (a + 1) * TILE, g * TILE : (g + 1) * TILE] = rows[
                            :, o * TILE : (o + 1) * TILE
                        ]

        @pl.loop(0, SECTORS)
        def _(d):
            if kind == 0:
                ops = jnp.concatenate([mix_ref[sector ^ d ^ g, g] for g in range(OPS)], axis=0)
            else:
                ops = pair_ref[...]
            res = jnp.dot(c_ref[d], ops, preferred_element_type=F32)
            sides = []
            for h in range(2):
                first = res[2 * h * TILE : (2 * h + 1) * TILE].reshape(16, 8, TILE)
                second = res[(2 * h + 1) * TILE : (2 * h + 2) * TILE].reshape(16, 8, TILE)
                sides.append(swap_halves(first, second))
            for o in range(2):
                both = jnp.concatenate([sides[0][o][:, None], sides[1][o][:, None]], axis=1)
                out_ref[d, :, o, kind] = both.reshape(16, 16, TILE).astype(BF)


def unpack_kernel(recv_ref, beta_ref, out_ref):
    order = deinterleave(512, 512)
    for t in range(TILES):
        cols = slice(t * TILE, (t + 1) * TILE)
        both = jnp.concatenate(
            [recv_ref[:, t, :, kind].reshape(512, TILE) for kind in range(2)], axis=1
        )
        moved = jnp.dot(order, both, preferred_element_type=F32)
        for p in range(ABLK):
            rows = slice(p * TILE, (p + 1) * TILE)
            out_ref[rows, cols] = beta_ref[rows, cols] + moved[rows, :TILE] + moved[rows, TILE:].T


def call(kernel, out_shape, scratch=()):
    return pl.pallas_call(
        kernel,
        out_shape=out_shape,
        scratch_shapes=list(scratch),
        compiler_params=pltpu.CompilerParams(vmem_limit_bytes=VMEM_BYTES),
    )


def signed_weights(source, sign, pair):
    key = pair * NBLK + source
    ids = jnp.arange(OPS * NBLK, dtype=jnp.int32)
    hit = key[:, :, None] == ids[None, None, :]
    factor = (1 - 2 * sign).astype(F32)
    return jnp.sum(jnp.where(hit, factor[:, :, None], 0.0), axis=1).astype(BF)


def swapped(array, mask):
    return lax.ppermute(array, "sym", [(s, s ^ mask) for s in range(SECTORS)])


def per_device(
    coeffs,
    beta_op,
    mix_op,
    pair_op,
    send_list,
    mix_slot,
    mix_sign,
    mix_pair,
    aa_src,
    aa_sign,
    aa_pair,
):
    tile = lax.axis_index("rows") // XDIM
    mine = lax.dynamic_index_in_dim(mix_op[0], tile, axis=1, keepdims=False)
    same = jnp.stack([mine] + [swapped(mine, k) for k in (2, 4, 6)])
    other = swapped(same, 1)

    send = call(
        pack_kernel, jax.ShapeDtypeStruct((SECTORS, TILES, XDIM, 2, 16, TILE), BF)
    )(coeffs)
    recv = lax.all_to_all(
        send.reshape(256, 32, TILE), ("sym", "rows"), split_axis=0, concat_axis=0, tiled=True
    )

    table = jnp.transpose(send_list, (1, 0, 2)).reshape(RANKS, RANKS * CAP)
    slots = jnp.arange(RANKS * CAP, dtype=jnp.int32)
    table = jnp.broadcast_to(table[:, None, :], (RANKS, ABLK, RANKS * CAP)).reshape(NBLK, 1, RANKS * CAP)
    owned = jnp.sum(jnp.where(mix_slot[:, :, None] == slots[None, None, :], table, 0), axis=2)
    source = (mix_slot // CAP) * ABLK + owned
    w_mix = signed_weights(source, mix_sign, mix_pair)
    w_alpha = signed_weights(aa_src, aa_sign, aa_pair)
    pairs = jnp.transpose(pair_op, (0, 2, 1)).reshape(OPS * TILE, TILE)

    back = call(
        middle_kernel,
        jax.ShapeDtypeStruct((SECTORS, 16, 2, 2, 16, TILE), BF),
        (
            pltpu.VMEM((SECTORS, ABLK, TILE, TILE), BF),
            pltpu.VMEM((SECTORS, 4 * TILE, OPS * TILE), BF),
            pltpu.VMEM((SECTORS, OPS, TILE, TILE), BF),
        ),
    )(recv.reshape(SECTORS, RANKS, 2, 16, TILE), same, other, pairs, w_mix, w_alpha)
    home = lax.all_to_all(
        back.reshape(256, 32, TILE), ("sym", "rows"), split_axis=0, concat_axis=0, tiled=True
    )
    beta_part = jnp.dot(coeffs, beta_op[0], preferred_element_type=F32)
    return call(unpack_kernel, jax.ShapeDtypeStruct(coeffs.shape, F32))(
        home.reshape(SECTORS, TILES, XDIM, 2, 16, TILE), beta_part
    )


def solution(mesh):
    in_specs = (
        P("rows", "sym"),
        P("sym", None, None),
        P("sym", None, None, None, None),
        P(),
        P(),
        P(),
        P(),
        P(),
        P(),
        P(),
        P(),
    )
    out_specs = P("rows", "sym")
    return jax.shard_map(
        per_device, mesh=mesh, in_specs=in_specs, out_specs=out_specs, check_vma=False
    )
```

```python
import jax
import jax.numpy as jnp
from jax import lax
from jax.experimental import pallas as pl
from jax.experimental.pallas import tpu as pltpu
from jax.sharding import Mesh, PartitionSpec as P

TILE = 128
ABLK = 4
CAP = 2
OPS = 8
SECTORS = 8
RANKS = 32
XDIM = 4
TILES = 8
NBLK = 128
BF = jnp.bfloat16
F32 = jnp.float32
VMEM_BYTES = 56 * 1024 * 1024


def interleave(rows, cols):
    r = lax.broadcasted_iota(jnp.int32, (rows, cols), 0)
    k = lax.broadcasted_iota(jnp.int32, (rows, cols), 1)
    return (k == (r % ABLK) * TILE + r // ABLK).astype(F32).astype(BF)


def deinterleave(rows, cols):
    r = lax.broadcasted_iota(jnp.int32, (rows, cols), 0)
    k = lax.broadcasted_iota(jnp.int32, (rows, cols), 1)
    return (r == (k % ABLK) * TILE + k // ABLK).astype(F32).astype(BF)


def pack_kernel(c_ref, send_ref):
    order = interleave(512, 512)
    for t in range(0, TILES, 2):
        turned = []
        for u in (t, t + 1):
            block = c_ref[:, u * TILE : (u + 1) * TILE].astype(F32)
            turned.append(
                jnp.concatenate(
                    [block[p * TILE : (p + 1) * TILE].T.astype(BF) for p in range(ABLK)], axis=0
                )
            )
        both = jnp.concatenate(turned, axis=1)
        moved = jnp.dot(order, both, preferred_element_type=F32).astype(BF)
        send_ref[t] = moved[:, :TILE]
        send_ref[t + 1] = moved[:, TILE:]


def swap_halves(first, second):
    low = lax.broadcasted_iota(jnp.int32, first.shape, 1) < 4
    lo = jnp.where(low, first, pltpu.roll(second, 4, 1))
    hi = jnp.where(low, pltpu.roll(first, 4, 1), second)
    return lo, hi


def blocks_of(recv_ref, c):
    got = recv_ref[:, c].astype(F32).reshape(16, 2, 2, 8, TILE)
    blocks = []
    for h in range(2):
        blocks += [b.reshape(TILE, TILE) for b in swap_halves(got[:, 0, h], got[:, 1, h])]
    return blocks


def regroup(blocks, out_ref, c):
    sides = []
    for h in range(2):
        first = blocks[2 * h].reshape(16, 8, TILE)
        second = blocks[2 * h + 1].reshape(16, 8, TILE)
        sides.append(swap_halves(first, second))
    for o in range(2):
        both = jnp.concatenate([sides[0][o][:, None], sides[1][o][:, None]], axis=1)
        out_ref[:, o, c] = both.reshape(16, 16, TILE).astype(BF)


def turn_kernel(recv_ref, out_ref):
    @pl.loop(0, TILES)
    def _(c):
        regroup([b.T for b in blocks_of(recv_ref, c)], out_ref, c)


def stacked(w_ref):
    return jnp.concatenate([w_ref[:, g * TILE : (g + 1) * TILE] for g in range(OPS)], axis=0)


def combine(weights, x_ref, c_ref, flip):
    @pl.loop(0, SECTORS // 2)
    def _(half):
        s = half * 2
        for a in range(ABLK):
            pair = jnp.concatenate([x_ref[s, a], x_ref[s + 1, a]], axis=1)
            combo = jnp.dot(weights, pair, preferred_element_type=F32).astype(BF)
            for g in range(OPS):
                rows = combo[g * TILE : (g + 1) * TILE]
                for o in range(2):
                    dest = (s + o) ^ g if flip else s + o
                    c_ref[dest, a * TILE : (a + 1) * TILE, g * TILE : (g + 1) * TILE] = rows[
                        :, o * TILE : (o + 1) * TILE
                    ]


def alpha_kernel(recv_ref, pair_ref, w_ref, out_ref, x_ref, c_ref):
    @pl.loop(0, SECTORS)
    def _(c):
        for a, block in enumerate(blocks_of(recv_ref, c)):
            x_ref[c, a] = block.astype(BF)

    combine(stacked(w_ref), x_ref, c_ref, False)

    @pl.loop(0, SECTORS)
    def _(c):
        res = jnp.dot(c_ref[c], pair_ref[...], preferred_element_type=F32)
        regroup([res[a * TILE : (a + 1) * TILE].T for a in range(ABLK)], out_ref, c)


def landed(land_ref, s, order):
    both = jnp.concatenate([land_ref[s], land_ref[s + 1]], axis=1)
    return jnp.dot(order, both, preferred_element_type=F32)


def mixed_kernel(land_ref, same_ref, other_ref, w_ref, res_ref, x_ref, c_ref, mix_ref):
    sector = lax.axis_index("sym")
    for k in range(SECTORS // 2):
        mix_ref[2 * k] = same_ref[k]
        mix_ref[2 * k + 1] = other_ref[k]
    order = deinterleave(512, 512)

    @pl.loop(0, SECTORS // 2)
    def _(half):
        moved = landed(land_ref, 2 * half, order)
        for a in range(ABLK):
            for o in range(2):
                block = moved[a * TILE : (a + 1) * TILE, o * TILE : (o + 1) * TILE]
                x_ref[2 * half + o, a] = block.T.astype(BF)

    combine(stacked(w_ref), x_ref, c_ref, True)

    @pl.loop(0, SECTORS)
    def _(d):
        ops = jnp.concatenate([mix_ref[sector ^ d ^ g, g] for g in range(OPS)], axis=0)
        res_ref[d] = jnp.dot(c_ref[d], ops, preferred_element_type=F32)


def merge_kernel(res_ref, land_ref, out_ref):
    order = deinterleave(512, 512)

    @pl.loop(0, SECTORS // 2)
    def _(half):
        moved = landed(land_ref, 2 * half, order)
        for o in range(2):
            d = 2 * half + o
            blocks = []
            for a in range(ABLK):
                rows = slice(a * TILE, (a + 1) * TILE)
                blocks.append(res_ref[d, rows] + moved[rows, o * TILE : (o + 1) * TILE].T)
            sides = []
            for h in range(2):
                first = blocks[2 * h].reshape(16, 8, TILE)
                second = blocks[2 * h + 1].reshape(16, 8, TILE)
                sides.append(swap_halves(first, second))
            for side in range(2):
                both = jnp.concatenate([sides[0][side][:, None], sides[1][side][:, None]], axis=1)
                out_ref[d, :, side] = both.reshape(16, 16, TILE).astype(BF)


def unpack_kernel(recv_ref, beta_ref, out_ref):
    order = deinterleave(512, 512)
    for t in range(0, TILES, 2):
        cols = slice(t * TILE, (t + 2) * TILE)
        both = jnp.concatenate(
            [recv_ref[:, u].reshape(512, TILE) for u in (t, t + 1)], axis=1
        )
        out_ref[:, cols] = beta_ref[:, cols] + jnp.dot(order, both, preferred_element_type=F32)


def call(kernel, out_shape, scratch=()):
    return pl.pallas_call(
        kernel,
        out_shape=out_shape,
        scratch_shapes=list(scratch),
        compiler_params=pltpu.CompilerParams(vmem_limit_bytes=VMEM_BYTES),
    )


def signed_weights(source, sign, pair):
    key = pair * NBLK + source
    ids = jnp.arange(OPS * NBLK, dtype=jnp.int32)
    hit = key[:, :, None] == ids[None, None, :]
    factor = (1 - 2 * sign).astype(F32)
    return jnp.sum(jnp.where(hit, factor[:, :, None], 0.0), axis=1).astype(BF)


def swapped(array, mask):
    return lax.ppermute(array, "sym", [(s, s ^ mask) for s in range(SECTORS)])


def per_device(
    coeffs,
    beta_op,
    mix_op,
    pair_op,
    send_list,
    mix_slot,
    mix_sign,
    mix_pair,
    aa_src,
    aa_sign,
    aa_pair,
):
    tile = lax.axis_index("z")
    mine = lax.dynamic_index_in_dim(mix_op[0], tile, axis=1, keepdims=False)
    same = jnp.stack([mine] + [swapped(mine, k) for k in (2, 4, 6)])
    other = swapped(same, 1)

    send = call(pack_kernel, jax.ShapeDtypeStruct((TILES, 512, TILE), BF))(coeffs)
    recv = exchange(send.reshape(32, TILE, TILE), ("z", "x"))
    recv = recv.reshape(RANKS, TILES, 16, TILE)
    grouped = jax.ShapeDtypeStruct((16, 2, TILES, 16, TILE), BF)
    turned = call(turn_kernel, grouped)(recv)
    land = exchange(turned.reshape(32, TILE, TILE), ("sym", "x"))

    table = jnp.transpose(send_list, (1, 0, 2)).reshape(RANKS, RANKS * CAP)
    slots = jnp.arange(RANKS * CAP, dtype=jnp.int32)
    table = jnp.broadcast_to(table[:, None, :], (RANKS, ABLK, RANKS * CAP)).reshape(NBLK, 1, RANKS * CAP)
    owned = jnp.sum(jnp.where(mix_slot[:, :, None] == slots[None, None, :], table, 0), axis=2)
    source = (mix_slot // CAP) * ABLK + owned
    w_mix = signed_weights(source, mix_sign, mix_pair)
    w_alpha = signed_weights(aa_src, aa_sign, aa_pair)
    pairs = jnp.transpose(pair_op, (0, 2, 1)).reshape(OPS * TILE, TILE)

    blocks = pltpu.VMEM((SECTORS, ABLK, TILE, TILE), BF)
    combos = pltpu.VMEM((SECTORS, 4 * TILE, OPS * TILE), BF)
    alpha = call(alpha_kernel, grouped, (blocks, combos))(recv, pairs, w_alpha)
    alpha_land = exchange(alpha.reshape(32, TILE, TILE), ("sym", "x"))
    mixed = call(
        mixed_kernel,
        jax.ShapeDtypeStruct((SECTORS, 512, TILE), F32),
        (blocks, combos, pltpu.VMEM((SECTORS, OPS, TILE, TILE), BF)),
    )(land.reshape(SECTORS, 512, TILE), same, other, w_mix)
    back = call(merge_kernel, jax.ShapeDtypeStruct((SECTORS, 16, 2, 16, TILE), BF))(
        mixed, alpha_land.reshape(SECTORS, 512, TILE)
    )
    home = exchange(back.reshape(256, 16, TILE), ("sym", "z", "x"))
    beta_part = jnp.dot(coeffs, beta_op[0], preferred_element_type=F32)
    return call(unpack_kernel, jax.ShapeDtypeStruct(coeffs.shape, F32))(
        home.reshape(SECTORS, TILES, XDIM, 16, TILE), beta_part
    )


def exchange(array, axes):
    return lax.all_to_all(array, axes, split_axis=0, concat_axis=0, tiled=True)


def solution(mesh):
    fine = Mesh(mesh.devices.reshape(SECTORS, TILES, XDIM), ("sym", "z", "x"))
    rows = ("z", "x")
    in_specs = (
        P(rows, "sym"),
        P("sym", None, None),
        P("sym", None, None, None, None),
        P(),
        P(),
        P(),
        P(),
        P(),
        P(),
        P(),
        P(),
    )
    out_specs = P(rows, "sym")
    return jax.shard_map(
        per_device, mesh=fine, in_specs=in_specs, out_specs=out_specs, check_vma=False
    )
```

```python
import jax
import jax.numpy as jnp
from jax import lax
from jax.experimental import pallas as pl
from jax.experimental.pallas import tpu as pltpu
from jax.sharding import Mesh, PartitionSpec as P

TILE = 128
ABLK = 4
CAP = 2
OPS = 8
SECTORS = 8
RANKS = 32
XDIM = 4
TILES = 8
NBLK = 128
BF = jnp.bfloat16
F32 = jnp.float32
VMEM_BYTES = 56 * 1024 * 1024


def interleave(rows, cols):
    r = lax.broadcasted_iota(jnp.int32, (rows, cols), 0)
    k = lax.broadcasted_iota(jnp.int32, (rows, cols), 1)
    return (k == (r % ABLK) * TILE + r // ABLK).astype(F32).astype(BF)


def deinterleave(rows, cols):
    r = lax.broadcasted_iota(jnp.int32, (rows, cols), 0)
    k = lax.broadcasted_iota(jnp.int32, (rows, cols), 1)
    return (r == (k % ABLK) * TILE + k // ABLK).astype(F32).astype(BF)


def pack_kernel(c_ref, send_ref):
    order = interleave(512, 512)
    for t in range(0, TILES, 2):
        turned = []
        for u in (t, t + 1):
            block = c_ref[:, u * TILE : (u + 1) * TILE].astype(F32)
            turned.append(
                jnp.concatenate(
                    [block[p * TILE : (p + 1) * TILE].T.astype(BF) for p in range(ABLK)], axis=0
                )
            )
        both = jnp.concatenate(turned, axis=1)
        moved = jnp.dot(order, both, preferred_element_type=F32).astype(BF)
        send_ref[t] = moved[:, :TILE]
        send_ref[t + 1] = moved[:, TILE:]


def swap_halves(first, second):
    low = lax.broadcasted_iota(jnp.int32, first.shape, 1) < 4
    lo = jnp.where(low, first, pltpu.roll(second, 4, 1))
    hi = jnp.where(low, pltpu.roll(first, 4, 1), second)
    return lo, hi


def blocks_of(recv_ref, c):
    got = recv_ref[:, c].astype(F32).reshape(16, 2, 2, 8, TILE)
    blocks = []
    for h in range(2):
        blocks += [b.reshape(TILE, TILE) for b in swap_halves(got[:, 0, h], got[:, 1, h])]
    return blocks


def regroup(blocks, out_ref, c):
    sides = []
    for h in range(2):
        first = blocks[2 * h].reshape(16, 8, TILE)
        second = blocks[2 * h + 1].reshape(16, 8, TILE)
        sides.append(swap_halves(first, second))
    for o in range(2):
        both = jnp.concatenate([sides[0][o][:, None], sides[1][o][:, None]], axis=1)
        out_ref[:, o, c] = both.reshape(16, 16, TILE).astype(BF)


def turn_kernel(recv_ref, out_ref):
    @pl.loop(0, TILES)
    def _(c):
        regroup([b.T for b in blocks_of(recv_ref, c)], out_ref, c)


def stacked(w_ref):
    return jnp.concatenate([w_ref[:, g * TILE : (g + 1) * TILE] for g in range(OPS)], axis=0)


def combine(weights, x_ref, c_ref, flip):
    @pl.loop(0, SECTORS // 2)
    def _(half):
        s = half * 2
        for a in range(ABLK):
            pair = jnp.concatenate([x_ref[s, a], x_ref[s + 1, a]], axis=1)
            combo = jnp.dot(weights, pair, preferred_element_type=F32).astype(BF)
            for g in range(OPS):
                rows = combo[g * TILE : (g + 1) * TILE]
                for o in range(2):
                    dest = (s + o) ^ g if flip else s + o
                    c_ref[dest, a * TILE : (a + 1) * TILE, g * TILE : (g + 1) * TILE] = rows[
                        :, o * TILE : (o + 1) * TILE
                    ]


def alpha_kernel(recv_ref, pair_ref, w_ref, out_ref, x_ref, c_ref):
    @pl.loop(0, SECTORS)
    def _(c):
        for a, block in enumerate(blocks_of(recv_ref, c)):
            x_ref[c, a] = block.astype(BF)

    combine(stacked(w_ref), x_ref, c_ref, False)

    @pl.loop(0, SECTORS)
    def _(c):
        res = jnp.dot(c_ref[c], pair_ref[...], preferred_element_type=F32)
        regroup([res[a * TILE : (a + 1) * TILE].T for a in range(ABLK)], out_ref, c)


def landed(land_ref, s, order):
    both = jnp.concatenate([land_ref[s], land_ref[s + 1]], axis=1)
    return jnp.dot(order, both, preferred_element_type=F32)


def mixed_kernel(land_ref, same_ref, other_ref, w_ref, res_ref, x_ref, c_ref, mix_ref):
    sector = lax.axis_index("sym")
    for k in range(SECTORS // 2):
        mix_ref[2 * k] = same_ref[k]
        mix_ref[2 * k + 1] = other_ref[k]
    order = deinterleave(512, 512)

    @pl.loop(0, SECTORS // 2)
    def _(half):
        moved = landed(land_ref, 2 * half, order)
        for a in range(ABLK):
            for o in range(2):
                block = moved[a * TILE : (a + 1) * TILE, o * TILE : (o + 1) * TILE]
                x_ref[2 * half + o, a] = block.T.astype(BF)

    combine(stacked(w_ref), x_ref, c_ref, True)

    @pl.loop(0, SECTORS)
    def _(d):
        ops = jnp.concatenate([mix_ref[sector ^ d ^ g, g] for g in range(OPS)], axis=0)
        res_ref[d] = jnp.dot(c_ref[d], ops, preferred_element_type=F32)


def merge_kernel(res_ref, land_ref, out_ref):
    order = deinterleave(512, 512)

    @pl.loop(0, SECTORS // 2)
    def _(half):
        moved = landed(land_ref, 2 * half, order)
        for o in range(2):
            d = 2 * half + o
            blocks = []
            for a in range(ABLK):
                rows = slice(a * TILE, (a + 1) * TILE)
                blocks.append(res_ref[d, rows] + moved[rows, o * TILE : (o + 1) * TILE].T)
            sides = []
            for h in range(2):
                first = blocks[2 * h].reshape(16, 8, TILE)
                second = blocks[2 * h + 1].reshape(16, 8, TILE)
                sides.append(swap_halves(first, second))
            for side in range(2):
                both = jnp.concatenate([sides[0][side][:, None], sides[1][side][:, None]], axis=1)
                out_ref[d, :, side] = both.reshape(16, 16, TILE).astype(BF)


def unpack_kernel(recv_ref, beta_ref, out_ref):
    order = deinterleave(512, 512)
    for t in range(0, TILES, 2):
        cols = slice(t * TILE, (t + 2) * TILE)
        both = jnp.concatenate(
            [recv_ref[:, u].reshape(512, TILE) for u in (t, t + 1)], axis=1
        )
        out_ref[:, cols] = beta_ref[:, cols] + jnp.dot(order, both, preferred_element_type=F32)


def call(kernel, out_shape, scratch=()):
    return pl.pallas_call(
        kernel,
        out_shape=out_shape,
        scratch_shapes=list(scratch),
        compiler_params=pltpu.CompilerParams(vmem_limit_bytes=VMEM_BYTES),
    )


def signed_weights(source, sign, pair):
    key = pair * NBLK + source
    ids = jnp.arange(OPS * NBLK, dtype=jnp.int32)
    hit = key[:, :, None] == ids[None, None, :]
    factor = (1 - 2 * sign).astype(F32)
    return jnp.sum(jnp.where(hit, factor[:, :, None], 0.0), axis=1).astype(BF)


def swapped(array, mask):
    return lax.ppermute(array, "sym", [(s, s ^ mask) for s in range(SECTORS)])


def per_device(
    coeffs,
    beta_op,
    mix_op,
    pair_op,
    send_list,
    mix_slot,
    mix_sign,
    mix_pair,
    aa_src,
    aa_sign,
    aa_pair,
):
    tile = lax.axis_index("z")
    mine = lax.dynamic_index_in_dim(mix_op[0], tile, axis=1, keepdims=False)
    same = jnp.stack([mine] + [swapped(mine, k) for k in (2, 4, 6)])
    other = swapped(same, 1)

    send = call(pack_kernel, jax.ShapeDtypeStruct((TILES, 512, TILE), BF))(coeffs)
    recv = exchange(send.reshape(32, TILE, TILE), ("z", "x"))
    table = jnp.transpose(send_list, (1, 0, 2)).reshape(RANKS, RANKS * CAP)
    slots = jnp.arange(RANKS * CAP, dtype=jnp.int32)
    table = jnp.broadcast_to(table[:, None, :], (RANKS, ABLK, RANKS * CAP)).reshape(NBLK, 1, RANKS * CAP)
    owned = jnp.sum(jnp.where(mix_slot[:, :, None] == slots[None, None, :], table, 0), axis=2)
    source = (mix_slot // CAP) * ABLK + owned
    w_mix = signed_weights(source, mix_sign, mix_pair)
    w_alpha = signed_weights(aa_src, aa_sign, aa_pair)
    pairs = jnp.transpose(pair_op, (0, 2, 1)).reshape(OPS * TILE, TILE)

    recv, same, other, w_mix, w_alpha, pairs = lax.optimization_barrier(
        (recv, same, other, w_mix, w_alpha, pairs)
    )
    recv = recv.reshape(RANKS, TILES, 16, TILE)
    grouped = jax.ShapeDtypeStruct((16, 2, TILES, 16, TILE), BF)
    turned = call(turn_kernel, grouped)(recv)
    land = exchange(turned.reshape(32, TILE, TILE), ("sym", "x"))

    blocks = pltpu.VMEM((SECTORS, ABLK, TILE, TILE), BF)
    combos = pltpu.VMEM((SECTORS, 4 * TILE, OPS * TILE), BF)
    alpha = call(alpha_kernel, grouped, (blocks, combos))(recv, pairs, w_alpha)
    alpha_land = exchange(alpha.reshape(32, TILE, TILE), ("sym", "x"))
    mixed = call(
        mixed_kernel,
        jax.ShapeDtypeStruct((SECTORS, 512, TILE), F32),
        (blocks, combos, pltpu.VMEM((SECTORS, OPS, TILE, TILE), BF)),
    )(land.reshape(SECTORS, 512, TILE), same, other, w_mix)
    back = call(merge_kernel, jax.ShapeDtypeStruct((SECTORS, 16, 2, 16, TILE), BF))(
        mixed, alpha_land.reshape(SECTORS, 512, TILE)
    )
    home = exchange(back.reshape(256, 16, TILE), ("sym", "z", "x"))
    beta_part = jnp.dot(coeffs, beta_op[0], preferred_element_type=F32)
    return call(unpack_kernel, jax.ShapeDtypeStruct(coeffs.shape, F32))(
        home.reshape(SECTORS, TILES, XDIM, 16, TILE), beta_part
    )


def exchange(array, axes):
    return lax.all_to_all(array, axes, split_axis=0, concat_axis=0, tiled=True)


def solution(mesh):
    fine = Mesh(mesh.devices.reshape(SECTORS, TILES, XDIM), ("sym", "z", "x"))
    rows = ("z", "x")
    in_specs = (
        P(rows, "sym"),
        P("sym", None, None),
        P("sym", None, None, None, None),
        P(),
        P(),
        P(),
        P(),
        P(),
        P(),
        P(),
        P(),
    )
    out_specs = P(rows, "sym")
    return jax.shard_map(
        per_device, mesh=fine, in_specs=in_specs, out_specs=out_specs, check_vma=False
    )
```

```python
import jax
import jax.numpy as jnp
from jax import lax
from jax.experimental import pallas as pl
from jax.experimental.pallas import tpu as pltpu
from jax.sharding import Mesh, PartitionSpec as P

TILE = 128
ABLK = 4
CAP = 2
OPS = 8
SECTORS = 8
RANKS = 32
XDIM = 4
TILES = 8
NBLK = 128
BF = jnp.bfloat16
F32 = jnp.float32
MIB = 1024 * 1024


def interleave(rows, cols):
    r = lax.broadcasted_iota(jnp.int32, (rows, cols), 0)
    k = lax.broadcasted_iota(jnp.int32, (rows, cols), 1)
    return (k == (r % ABLK) * TILE + r // ABLK).astype(F32).astype(BF)


def deinterleave(rows, cols):
    r = lax.broadcasted_iota(jnp.int32, (rows, cols), 0)
    k = lax.broadcasted_iota(jnp.int32, (rows, cols), 1)
    return (r == (k % ABLK) * TILE + k // ABLK).astype(F32).astype(BF)


def pack_kernel(c_hbm, send_hbm, c_ref, t_ref, send_ref, in_sem, out_sem):
    loads = []
    for p in range(ABLK):
        rows = pl.ds(p * TILE, TILE)
        loads.append(pltpu.make_async_copy(c_hbm.at[rows], c_ref.at[rows], in_sem.at[p]))
        loads[-1].start()
    order = interleave(512, 512)
    for p in range(ABLK):
        loads[p].wait()
        for t in range(TILES):
            block = c_ref[p * TILE : (p + 1) * TILE, t * TILE : (t + 1) * TILE].astype(F32)
            t_ref[p * TILE : (p + 1) * TILE, t * TILE : (t + 1) * TILE] = block.T.astype(BF)
    stores = []
    for k in range(4):
        both = t_ref[:, k * 2 * TILE : (k + 1) * 2 * TILE]
        moved = jnp.dot(order, both, preferred_element_type=F32).astype(BF)
        for o in range(2):
            part = moved[:, o * TILE : (o + 1) * TILE]
            send_ref[:, 2 * k + o] = part.reshape(XDIM, TILE, TILE)
        here = pl.ds(2 * k, 2)
        stores.append(
            pltpu.make_async_copy(send_ref.at[:, here], send_hbm.at[:, here], out_sem.at[k])
        )
        stores[-1].start()
    for copy in stores:
        copy.wait()


def swap_halves(first, second):
    low = lax.broadcasted_iota(jnp.int32, first.shape, 1) < 4
    lo = jnp.where(low, first, pltpu.roll(second, 4, 1))
    hi = jnp.where(low, pltpu.roll(first, 4, 1), second)
    return lo, hi


def blocks_of(recv_ref, c):
    got = recv_ref[:, c].astype(F32).reshape(16, 2, 2, 8, TILE)
    blocks = []
    for h in range(2):
        blocks += [b.reshape(TILE, TILE) for b in swap_halves(got[:, 0, h], got[:, 1, h])]
    return blocks


def regroup(blocks, out_ref, c):
    sides = []
    for h in range(2):
        first = blocks[2 * h].reshape(16, 8, TILE)
        second = blocks[2 * h + 1].reshape(16, 8, TILE)
        sides.append(swap_halves(first, second))
    for o in range(2):
        both = jnp.concatenate([sides[0][o][:, None], sides[1][o][:, None]], axis=1)
        out_ref[:, o, c] = both.reshape(16, 16, TILE).astype(BF)


def turn_kernel(recv_ref, out_hbm, out_ref, out_sem):
    stores = []
    for c in range(TILES):
        regroup([b.T for b in blocks_of(recv_ref, c)], out_ref, c)
        stores.append(
            pltpu.make_async_copy(out_ref.at[:, :, c], out_hbm.at[:, :, c], out_sem.at[c])
        )
        stores[-1].start()
    for copy in stores:
        copy.wait()


def stacked(w_ref):
    return jnp.concatenate([w_ref[:, g * TILE : (g + 1) * TILE] for g in range(OPS)], axis=0)


def combine(weights, x_ref, c_ref, flip):
    @pl.loop(0, SECTORS // 2)
    def _(half):
        s = half * 2
        for a in range(ABLK):
            pair = jnp.concatenate([x_ref[s, a], x_ref[s + 1, a]], axis=1)
            combo = jnp.dot(weights, pair, preferred_element_type=F32).astype(BF)
            for g in range(OPS):
                rows = combo[g * TILE : (g + 1) * TILE]
                for o in range(2):
                    dest = (s + o) ^ g if flip else s + o
                    c_ref[dest, a * TILE : (a + 1) * TILE, g * TILE : (g + 1) * TILE] = rows[
                        :, o * TILE : (o + 1) * TILE
                    ]


def alpha_kernel(recv_ref, pair_ref, w_ref, out_ref, x_ref, c_ref):
    @pl.loop(0, SECTORS)
    def _(c):
        for a, block in enumerate(blocks_of(recv_ref, c)):
            x_ref[c, a] = block.astype(BF)

    combine(stacked(w_ref), x_ref, c_ref, False)

    @pl.loop(0, SECTORS)
    def _(c):
        res = jnp.dot(c_ref[c], pair_ref[...], preferred_element_type=F32)
        regroup([res[a * TILE : (a + 1) * TILE].T for a in range(ABLK)], out_ref, c)


def landed(land_ref, s, order):
    both = jnp.concatenate([land_ref[:, s + o].reshape(512, TILE) for o in range(2)], axis=1)
    return jnp.dot(order, both, preferred_element_type=F32)


def mixed_kernel(
    land_ref, o0, o1, o2, o3, o4, o5, o6, o7, w_ref, res_hbm, x_ref, c_ref, mix_ref, res_ref, out_sem
):
    sector = lax.axis_index("sym")
    for k, op_ref in enumerate((o0, o1, o2, o3, o4, o5, o6, o7)):
        mix_ref[k] = op_ref[...]
    order = deinterleave(512, 512)

    @pl.loop(0, SECTORS // 2)
    def _(half):
        moved = landed(land_ref, 2 * half, order)
        for a in range(ABLK):
            for o in range(2):
                block = moved[a * TILE : (a + 1) * TILE, o * TILE : (o + 1) * TILE]
                x_ref[2 * half + o, a] = block.T.astype(BF)

    combine(stacked(w_ref), x_ref, c_ref, True)

    @pl.loop(0, SECTORS)
    def _(d):
        ops = jnp.concatenate([mix_ref[sector ^ d ^ g, g] for g in range(OPS)], axis=0)
        res_ref[d] = jnp.dot(c_ref[d], ops, preferred_element_type=F32)
        pltpu.make_async_copy(res_ref.at[d], res_hbm.at[d], out_sem.at[d]).start()

    @pl.loop(0, SECTORS)
    def _(d):
        pltpu.make_async_copy(res_ref.at[d], res_hbm.at[d], out_sem.at[d]).wait()


def merge_kernel(
    res_hbm, land_hbm, out_hbm, res_ref, land_ref, out_ref, in_sem, land_sem, out_sem
):
    loads, lands = [], []
    for half in range(SECTORS // 2):
        here = pl.ds(2 * half, 2)
        lands.append(
            pltpu.make_async_copy(land_hbm.at[:, here], land_ref.at[:, here], land_sem.at[half])
        )
        loads.append(
            pltpu.make_async_copy(res_hbm.at[here], res_ref.at[here], in_sem.at[half])
        )
        lands[-1].start()
        loads[-1].start()
    order = deinterleave(512, 512)
    stores = []
    for half in range(SECTORS // 2):
        lands[half].wait()
        moved = landed(land_ref, 2 * half, order)
        loads[half].wait()
        for o in range(2):
            d = 2 * half + o
            blocks = []
            for a in range(ABLK):
                rows = slice(a * TILE, (a + 1) * TILE)
                blocks.append(res_ref[d, rows] + moved[rows, o * TILE : (o + 1) * TILE].T)
            sides = []
            for h in range(2):
                first = blocks[2 * h].reshape(16, 8, TILE)
                second = blocks[2 * h + 1].reshape(16, 8, TILE)
                sides.append(swap_halves(first, second))
            for side in range(2):
                both = jnp.concatenate([sides[0][side][:, None], sides[1][side][:, None]], axis=1)
                both = both.reshape(TILES, 2, 16, TILE).astype(BF)
                for v in range(2):
                    out_ref[2 * v + side, d] = both[:, v]
            stores.append(
                pltpu.make_async_copy(out_ref.at[:, d], out_hbm.at[:, d], out_sem.at[d])
            )
            stores[-1].start()
    for copy in stores:
        copy.wait()


def beta_kernel(c_hbm, op_hbm, out_hbm, c_ref, op_ref, out_ref, in_sem, out_sem):
    loads = [
        pltpu.make_async_copy(c_hbm, c_ref, in_sem.at[0]),
        pltpu.make_async_copy(op_hbm, op_ref, in_sem.at[1]),
    ]
    for copy in loads:
        copy.start()
    for copy in loads:
        copy.wait()
    for k in range(4):
        cols = slice(k * 2 * TILE, (k + 1) * 2 * TILE)
        out_ref[:, cols] = jnp.dot(c_ref[...], op_ref[:, cols], preferred_element_type=F32)
    store = pltpu.make_async_copy(out_ref, out_hbm, out_sem)
    store.start()
    store.wait()


def unpack_kernel(recv_ref, beta_hbm, out_hbm, beta_ref, out_ref, in_sem, out_sem):
    loads = []
    for k in range(4):
        cols = pl.ds(k * 2 * TILE, 2 * TILE)
        loads.append(
            pltpu.make_async_copy(beta_hbm.at[:, cols], beta_ref.at[:, cols], in_sem.at[k])
        )
        loads[-1].start()
    order = deinterleave(512, 512)
    stores = []
    for k in range(4):
        both = jnp.concatenate(
            [recv_ref[:, :, u].reshape(512, TILE) for u in (2 * k, 2 * k + 1)], axis=1
        )
        moved = jnp.dot(order, both, preferred_element_type=F32)
        loads[k].wait()
        cols = pl.ds(k * 2 * TILE, 2 * TILE)
        out_ref[:, cols] = beta_ref[:, cols] + moved
        stores.append(
            pltpu.make_async_copy(out_ref.at[:, cols], out_hbm.at[:, cols], out_sem.at[k])
        )
        stores[-1].start()
    for copy in stores:
        copy.wait()


HBM, VMEM = pltpu.HBM, pltpu.VMEM


def call(kernel, out_shape, mib, ins, out, scratch):
    if out is HBM:
        out_shape = HBM(out_shape.shape, out_shape.dtype)
    run = pl.pallas_call(
        kernel,
        out_shape=out_shape,
        in_specs=[pl.BlockSpec(memory_space=place) for place in ins],
        out_specs=pl.BlockSpec(memory_space=out),
        scratch_shapes=scratch,
        compiler_params=pltpu.CompilerParams(vmem_limit_bytes=mib * MIB),
    )

    def placed(*args):
        return run(
            *(
                pltpu.with_memory_space_constraint(x, HBM) if place is HBM else x
                for x, place in zip(args, ins)
            )
        )

    return placed


def sems(count):
    return pltpu.SemaphoreType.DMA((count,))


def signed_weights(source, sign, pair):
    key = pair * NBLK + source
    ids = jnp.arange(OPS * NBLK, dtype=jnp.int32)
    hit = key[:, :, None] == ids[None, None, :]
    factor = (1 - 2 * sign).astype(F32)
    return jnp.sum(jnp.where(hit, factor[:, :, None], 0.0), axis=1).astype(BF)


def swapped(array, mask):
    return lax.ppermute(array, "sym", [(s, s ^ mask) for s in range(SECTORS)])


def per_device(
    coeffs,
    beta_op,
    mix_op,
    pair_op,
    send_list,
    mix_slot,
    mix_sign,
    mix_pair,
    aa_src,
    aa_sign,
    aa_pair,
):
    tile = lax.axis_index("z")
    mine = lax.dynamic_index_in_dim(mix_op[0], tile, axis=1, keepdims=False)
    ops = {0: mine}
    for k in (2, 4, 6, 1):
        ops[k] = swapped(mine, k)

    sent = (XDIM, TILES, TILE, TILE)
    send = call(
        pack_kernel,
        jax.ShapeDtypeStruct(sent, BF),
        8,
        [HBM],
        HBM,
        [pltpu.VMEM((512, 1024), BF)] * 2 + [pltpu.VMEM(sent, BF), sems(4), sems(4)],
    )(coeffs)
    recv = exchange(send.reshape(32, TILE, TILE), ("x", "z"))

    table = jnp.transpose(send_list, (1, 0, 2)).reshape(RANKS, RANKS * CAP)
    slots = jnp.arange(RANKS * CAP, dtype=jnp.int32)
    table = jnp.broadcast_to(table[:, None, :], (RANKS, ABLK, RANKS * CAP)).reshape(NBLK, 1, RANKS * CAP)
    owned = jnp.sum(jnp.where(mix_slot[:, :, None] == slots[None, None, :], table, 0), axis=2)
    source = (mix_slot // CAP) * ABLK + owned
    w_mix = signed_weights(arrival(source), mix_sign, mix_pair)
    w_alpha = signed_weights(arrival(aa_src), aa_sign, aa_pair)
    pairs = jnp.transpose(pair_op, (0, 2, 1)).reshape(OPS * TILE, TILE)
    ops[2], ops[4], ops[6], w_mix, w_alpha, pairs = lax.optimization_barrier(
        (ops[2], ops[4], ops[6], w_mix, w_alpha, pairs)
    )
    for k in (2, 4, 6):
        ops[k + 1] = swapped(ops[k], 1)
    held = [ops[k] for k in range(SECTORS)]
    recv, held, w_mix, w_alpha, pairs = lax.optimization_barrier(
        (recv, held, w_mix, w_alpha, pairs)
    )
    recv = recv.reshape(RANKS, TILES, 16, TILE)
    parted = (16, 2, TILES, 16, TILE)
    grouped = jax.ShapeDtypeStruct(parted, BF)
    turned = call(turn_kernel, grouped, 6, [VMEM], HBM, [pltpu.VMEM(parted, BF), sems(8)])(recv)
    land = exchange(turned.reshape(32, TILE, TILE), ("x", "sym"))

    blocks = pltpu.VMEM((SECTORS, ABLK, TILE, TILE), BF)
    combos = pltpu.VMEM((SECTORS, 4 * TILE, OPS * TILE), BF)
    alpha = call(alpha_kernel, grouped, 18, [VMEM] * 3, VMEM, [blocks, combos])(
        recv, pairs, w_alpha
    )
    alpha_land = exchange(alpha.reshape(32, TILE, TILE), ("x", "sym"))
    landing = (XDIM, SECTORS, TILE, TILE)
    result = (SECTORS, 512, TILE)
    mixed = call(
        mixed_kernel,
        jax.ShapeDtypeStruct(result, F32),
        24,
        [VMEM] * 10,
        HBM,
        [
            blocks,
            combos,
            pltpu.VMEM((SECTORS, OPS, TILE, TILE), BF),
            pltpu.VMEM(result, F32),
            sems(8),
        ],
    )(land.reshape(landing), *held, w_mix)
    out = (XDIM, SECTORS, TILES, 16, TILE)
    back = call(
        merge_kernel,
        jax.ShapeDtypeStruct(out, BF),
        12,
        [HBM, HBM],
        HBM,
        [
            pltpu.VMEM(result, F32),
            pltpu.VMEM(landing, BF),
            pltpu.VMEM(out, BF),
            sems(4),
            sems(4),
            sems(8),
        ],
    )(mixed, alpha_land.reshape(landing))
    back, later, beta_late = lax.optimization_barrier((back, coeffs, beta_op[0]))
    home = exchange(back.reshape(256, 16, TILE), ("x", "sym", "z"))
    beta_part = call(
        beta_kernel,
        jax.ShapeDtypeStruct(coeffs.shape, F32),
        12,
        [HBM, HBM],
        HBM,
        [
            pltpu.VMEM(coeffs.shape, BF),
            pltpu.VMEM(beta_late.shape, BF),
            pltpu.VMEM(coeffs.shape, F32),
            sems(2),
            pltpu.SemaphoreType.DMA,
        ],
    )(later, beta_late)
    return call(
        unpack_kernel,
        jax.ShapeDtypeStruct(coeffs.shape, F32),
        12,
        [VMEM, HBM],
        HBM,
        [pltpu.VMEM(coeffs.shape, F32), pltpu.VMEM(coeffs.shape, F32), sems(4), sems(4)],
    )(home.reshape(out), beta_part)


def arrival(block):
    rank = block // ABLK
    return ((rank % XDIM) * TILES + rank // XDIM) * ABLK + block % ABLK


def exchange(array, axes):
    return lax.all_to_all(array, axes, split_axis=0, concat_axis=0, tiled=True)


def solution(mesh):
    fine = Mesh(mesh.devices.reshape(SECTORS, TILES, XDIM), ("sym", "z", "x"))
    rows = ("z", "x")
    in_specs = (
        P(rows, "sym"),
        P("sym", None, None),
        P("sym", None, None, None, None),
        P(),
        P(),
        P(),
        P(),
        P(),
        P(),
        P(),
        P(),
    )
    out_specs = P(rows, "sym")
    return jax.shard_map(
        per_device, mesh=fine, in_specs=in_specs, out_specs=out_specs, check_vma=False
    )
```

```python
import jax
import jax.numpy as jnp
from jax import lax
from jax.experimental import pallas as pl
from jax.experimental.pallas import tpu as pltpu
from jax.sharding import Mesh, PartitionSpec as P

TILE = 128
ABLK = 4
CAP = 2
OPS = 8
SECTORS = 8
RANKS = 32
XDIM = 4
TILES = 8
NBLK = 128
BF = jnp.bfloat16
F32 = jnp.float32
MIB = 1024 * 1024


def interleave(rows, cols):
    r = lax.broadcasted_iota(jnp.int32, (rows, cols), 0)
    k = lax.broadcasted_iota(jnp.int32, (rows, cols), 1)
    return (k == (r % ABLK) * TILE + r // ABLK).astype(F32).astype(BF)


def deinterleave(rows, cols):
    r = lax.broadcasted_iota(jnp.int32, (rows, cols), 0)
    k = lax.broadcasted_iota(jnp.int32, (rows, cols), 1)
    return (r == (k % ABLK) * TILE + k // ABLK).astype(F32).astype(BF)


def pack_kernel(c_hbm, send_hbm, c_ref, t_ref, send_ref, in_sem, out_sem):
    loads = []
    for p in range(ABLK):
        rows = pl.ds(p * TILE, TILE)
        loads.append(pltpu.make_async_copy(c_hbm.at[rows], c_ref.at[rows], in_sem.at[p]))
        loads[-1].start()
    order = interleave(512, 512)
    for p in range(ABLK):
        loads[p].wait()
        for t in range(TILES):
            block = c_ref[p * TILE : (p + 1) * TILE, t * TILE : (t + 1) * TILE].astype(F32)
            t_ref[p * TILE : (p + 1) * TILE, t * TILE : (t + 1) * TILE] = block.T.astype(BF)
    stores = []
    for k in range(4):
        both = t_ref[:, k * 2 * TILE : (k + 1) * 2 * TILE]
        moved = jnp.dot(order, both, preferred_element_type=F32).astype(BF)
        for o in range(2):
            part = moved[:, o * TILE : (o + 1) * TILE]
            send_ref[:, 2 * k + o] = part.reshape(XDIM, TILE, TILE)
        here = pl.ds(2 * k, 2)
        stores.append(
            pltpu.make_async_copy(send_ref.at[:, here], send_hbm.at[:, here], out_sem.at[k])
        )
        stores[-1].start()
    for copy in stores:
        copy.wait()


def pick_kernel(op_hbm, out_hbm, op_ref, in_sem, out_sem):
    tile = lax.axis_index("z")
    load = pltpu.make_async_copy(op_hbm.at[0, :, tile], op_ref, in_sem)
    load.start()
    load.wait()
    store = pltpu.make_async_copy(op_ref, out_hbm, out_sem)
    store.start()
    store.wait()


def swap_halves(first, second):
    low = lax.broadcasted_iota(jnp.int32, first.shape, 1) < 4
    lo = jnp.where(low, first, pltpu.roll(second, 4, 1))
    hi = jnp.where(low, pltpu.roll(first, 4, 1), second)
    return lo, hi


def blocks_of(recv_ref, c):
    got = recv_ref[:, c].astype(F32).reshape(16, 2, 2, 8, TILE)
    blocks = []
    for h in range(2):
        blocks += [b.reshape(TILE, TILE) for b in swap_halves(got[:, 0, h], got[:, 1, h])]
    return blocks


def regroup(blocks, out_ref, c):
    sides = []
    for h in range(2):
        first = blocks[2 * h].reshape(16, 8, TILE)
        second = blocks[2 * h + 1].reshape(16, 8, TILE)
        sides.append(swap_halves(first, second))
    for o in range(2):
        both = jnp.concatenate([sides[0][o][:, None], sides[1][o][:, None]], axis=1)
        out_ref[:, o, c] = both.reshape(16, 16, TILE).astype(BF)


def turn_kernel(recv_ref, out_hbm, out_ref, out_sem):
    stores = []
    for c in range(TILES):
        regroup([b.T for b in blocks_of(recv_ref, c)], out_ref, c)
        stores.append(
            pltpu.make_async_copy(out_ref.at[:, :, c], out_hbm.at[:, :, c], out_sem.at[c])
        )
        stores[-1].start()
    for copy in stores:
        copy.wait()


def stacked(w_ref):
    return jnp.concatenate([w_ref[:, g * TILE : (g + 1) * TILE] for g in range(OPS)], axis=0)


def combine(weights, x_ref, c_ref, flip):
    @pl.loop(0, SECTORS // 2)
    def _(half):
        s = half * 2
        for a in range(ABLK):
            pair = jnp.concatenate([x_ref[s, a], x_ref[s + 1, a]], axis=1)
            combo = jnp.dot(weights, pair, preferred_element_type=F32).astype(BF)
            for g in range(OPS):
                rows = combo[g * TILE : (g + 1) * TILE]
                for o in range(2):
                    dest = (s + o) ^ g if flip else s + o
                    c_ref[dest, a * TILE : (a + 1) * TILE, g * TILE : (g + 1) * TILE] = rows[
                        :, o * TILE : (o + 1) * TILE
                    ]


def alpha_kernel(recv_ref, pair_ref, w_ref, out_ref, x_ref, c_ref):
    @pl.loop(0, SECTORS)
    def _(c):
        for a, block in enumerate(blocks_of(recv_ref, c)):
            x_ref[c, a] = block.astype(BF)

    combine(stacked(w_ref), x_ref, c_ref, False)

    @pl.loop(0, SECTORS)
    def _(c):
        res = jnp.dot(c_ref[c], pair_ref[...], preferred_element_type=F32)
        regroup([res[a * TILE : (a + 1) * TILE].T for a in range(ABLK)], out_ref, c)


def landed(land_ref, s, order):
    both = jnp.concatenate([land_ref[:, s + o].reshape(512, TILE) for o in range(2)], axis=1)
    return jnp.dot(order, both, preferred_element_type=F32)


def mixed_kernel(
    land_hbm, o0, o1, o2, o3, o4, o5, o6, o7, w_ref, res_hbm,
    land_ref, x_ref, c_ref, mix_ref, res_ref, land_sem, op_sem, out_sem,
):
    sector = lax.axis_index("sym")
    lands, loads = [], []
    for half in range(SECTORS // 2):
        here = pl.ds(2 * half, 2)
        lands.append(
            pltpu.make_async_copy(land_hbm.at[:, here], land_ref.at[:, here], land_sem.at[half])
        )
        lands[-1].start()
    for k, op_hbm in enumerate((o0, o1, o2, o3, o4, o5, o6, o7)):
        loads.append(pltpu.make_async_copy(op_hbm, mix_ref.at[k], op_sem.at[k]))
        loads[-1].start()
    order = deinterleave(512, 512)
    for half in range(SECTORS // 2):
        lands[half].wait()
        moved = landed(land_ref, 2 * half, order)
        for a in range(ABLK):
            for o in range(2):
                block = moved[a * TILE : (a + 1) * TILE, o * TILE : (o + 1) * TILE]
                x_ref[2 * half + o, a] = block.T.astype(BF)

    combine(stacked(w_ref), x_ref, c_ref, True)
    for copy in loads:
        copy.wait()

    @pl.loop(0, SECTORS)
    def _(d):
        ops = jnp.concatenate([mix_ref[sector ^ d ^ g, g] for g in range(OPS)], axis=0)
        res_ref[d] = jnp.dot(c_ref[d], ops, preferred_element_type=F32).astype(BF)
        pltpu.make_async_copy(res_ref.at[d], res_hbm.at[d], out_sem.at[d]).start()

    @pl.loop(0, SECTORS)
    def _(d):
        pltpu.make_async_copy(res_ref.at[d], res_hbm.at[d], out_sem.at[d]).wait()


def merge_kernel(res_hbm, land_ref, out_hbm, res_ref, out_ref, in_sem, out_sem):
    loads = []
    for half in range(SECTORS // 2):
        here = pl.ds(2 * half, 2)
        loads.append(
            pltpu.make_async_copy(res_hbm.at[here], res_ref.at[here], in_sem.at[half])
        )
        loads[-1].start()
    order = deinterleave(512, 512)
    stores = []
    for half in range(SECTORS // 2):
        moved = landed(land_ref, 2 * half, order)
        loads[half].wait()
        for o in range(2):
            d = 2 * half + o
            blocks = []
            for a in range(ABLK):
                rows = slice(a * TILE, (a + 1) * TILE)
                blocks.append(res_ref[d, rows].astype(F32) + moved[rows, o * TILE : (o + 1) * TILE].T)
            sides = []
            for h in range(2):
                first = blocks[2 * h].reshape(16, 8, TILE)
                second = blocks[2 * h + 1].reshape(16, 8, TILE)
                sides.append(swap_halves(first, second))
            for side in range(2):
                both = jnp.concatenate([sides[0][side][:, None], sides[1][side][:, None]], axis=1)
                both = both.reshape(TILES, 2, 16, TILE).astype(BF)
                for v in range(2):
                    out_ref[2 * v + side, d] = both[:, v]
            stores.append(
                pltpu.make_async_copy(out_ref.at[:, d], out_hbm.at[:, d], out_sem.at[d])
            )
            stores[-1].start()
    for copy in stores:
        copy.wait()


def beta_kernel(c_hbm, op_hbm, out_hbm, c_ref, op_ref, out_ref, in_sem, out_sem):
    loads = [
        pltpu.make_async_copy(c_hbm, c_ref, in_sem.at[0]),
        pltpu.make_async_copy(op_hbm, op_ref, in_sem.at[1]),
    ]
    for copy in loads:
        copy.start()
    for copy in loads:
        copy.wait()
    for k in range(4):
        cols = slice(k * 2 * TILE, (k + 1) * 2 * TILE)
        out_ref[:, cols] = jnp.dot(c_ref[...], op_ref[:, cols], preferred_element_type=F32)
    store = pltpu.make_async_copy(out_ref, out_hbm, out_sem)
    store.start()
    store.wait()


def unpack_kernel(recv_ref, beta_hbm, out_hbm, beta_ref, out_ref, in_sem, out_sem):
    loads = []
    for k in range(4):
        cols = pl.ds(k * 2 * TILE, 2 * TILE)
        loads.append(
            pltpu.make_async_copy(beta_hbm.at[:, cols], beta_ref.at[:, cols], in_sem.at[k])
        )
        loads[-1].start()
    order = deinterleave(512, 512)
    stores = []
    for k in range(4):
        both = jnp.concatenate(
            [recv_ref[:, :, u].reshape(512, TILE) for u in (2 * k, 2 * k + 1)], axis=1
        )
        moved = jnp.dot(order, both, preferred_element_type=F32)
        loads[k].wait()
        cols = pl.ds(k * 2 * TILE, 2 * TILE)
        out_ref[:, cols] = beta_ref[:, cols] + moved
        stores.append(
            pltpu.make_async_copy(out_ref.at[:, cols], out_hbm.at[:, cols], out_sem.at[k])
        )
        stores[-1].start()
    for copy in stores:
        copy.wait()


HBM, VMEM = pltpu.HBM, pltpu.VMEM


def call(kernel, out_shape, mib, ins, out, scratch):
    if out is HBM:
        out_shape = HBM(out_shape.shape, out_shape.dtype)
    run = pl.pallas_call(
        kernel,
        out_shape=out_shape,
        in_specs=[pl.BlockSpec(memory_space=place) for place in ins],
        out_specs=pl.BlockSpec(memory_space=out),
        scratch_shapes=scratch,
        compiler_params=pltpu.CompilerParams(vmem_limit_bytes=mib * MIB),
    )

    def placed(*args):
        return run(
            *(
                pltpu.with_memory_space_constraint(x, HBM) if place is HBM else x
                for x, place in zip(args, ins)
            )
        )

    return placed


def sems(count):
    return pltpu.SemaphoreType.DMA((count,))


def signed_weights(source, sign, pair):
    key = pair * NBLK + source
    ids = jnp.arange(OPS * NBLK, dtype=jnp.int32)
    hit = key[:, :, None] == ids[None, None, :]
    factor = (1 - 2 * sign).astype(F32)
    return jnp.sum(jnp.where(hit, factor[:, :, None], 0.0), axis=1).astype(BF)


def swapped(array, mask):
    return lax.ppermute(array, "sym", [(s, s ^ mask) for s in range(SECTORS)])


def per_device(
    coeffs,
    beta_op,
    mix_op,
    pair_op,
    send_list,
    mix_slot,
    mix_sign,
    mix_pair,
    aa_src,
    aa_sign,
    aa_pair,
):
    sent = (XDIM, TILES, TILE, TILE)
    send = call(
        pack_kernel,
        jax.ShapeDtypeStruct(sent, BF),
        8,
        [HBM],
        HBM,
        [pltpu.VMEM((512, 1024), BF)] * 2 + [pltpu.VMEM(sent, BF), sems(4), sems(4)],
    )(coeffs)
    send, picked = lax.optimization_barrier((send, mix_op))
    mine = call(
        pick_kernel,
        jax.ShapeDtypeStruct((OPS, TILE, TILE), BF),
        4,
        [HBM],
        HBM,
        [pltpu.VMEM((OPS, TILE, TILE), BF), pltpu.SemaphoreType.DMA, pltpu.SemaphoreType.DMA],
    )(picked)
    ops = {0: mine}
    for k in (2, 4, 6, 1):
        ops[k] = swapped(mine, k)
    recv = exchange(send.reshape(32, TILE, TILE), ("x", "z"))

    table = jnp.transpose(send_list, (1, 0, 2)).reshape(RANKS, RANKS * CAP)
    slots = jnp.arange(RANKS * CAP, dtype=jnp.int32)
    table = jnp.broadcast_to(table[:, None, :], (RANKS, ABLK, RANKS * CAP)).reshape(NBLK, 1, RANKS * CAP)
    owned = jnp.sum(jnp.where(mix_slot[:, :, None] == slots[None, None, :], table, 0), axis=2)
    source = (mix_slot // CAP) * ABLK + owned
    w_mix = signed_weights(arrival(source), mix_sign, mix_pair)
    w_alpha = signed_weights(arrival(aa_src), aa_sign, aa_pair)
    pairs = jnp.transpose(pair_op, (0, 2, 1)).reshape(OPS * TILE, TILE)
    ops[2], ops[4], ops[6], w_mix, w_alpha, pairs = lax.optimization_barrier(
        (ops[2], ops[4], ops[6], w_mix, w_alpha, pairs)
    )
    for k in (2, 4, 6):
        ops[k + 1] = swapped(ops[k], 1)
    held = [ops[k] for k in range(SECTORS)]
    recv, held, w_mix, w_alpha, pairs = lax.optimization_barrier(
        (recv, held, w_mix, w_alpha, pairs)
    )
    recv = recv.reshape(RANKS, TILES, 16, TILE)
    parted = (16, 2, TILES, 16, TILE)
    grouped = jax.ShapeDtypeStruct(parted, BF)
    turned = call(turn_kernel, grouped, 6, [VMEM], HBM, [pltpu.VMEM(parted, BF), sems(8)])(recv)
    land = exchange(turned.reshape(32, TILE, TILE), ("x", "sym"))

    blocks = pltpu.VMEM((SECTORS, ABLK, TILE, TILE), BF)
    combos = pltpu.VMEM((SECTORS, 4 * TILE, OPS * TILE), BF)
    alpha = call(alpha_kernel, grouped, 18, [VMEM] * 3, VMEM, [blocks, combos])(
        recv, pairs, w_alpha
    )
    alpha_land = exchange(alpha.reshape(32, TILE, TILE), ("x", "sym"))
    landing = (XDIM, SECTORS, TILE, TILE)
    result = (SECTORS, 512, TILE)
    mixed = call(
        mixed_kernel,
        jax.ShapeDtypeStruct(result, BF),
        24,
        [HBM] * 9 + [VMEM],
        HBM,
        [
            pltpu.VMEM(landing, BF),
            blocks,
            combos,
            pltpu.VMEM((SECTORS, OPS, TILE, TILE), BF),
            pltpu.VMEM(result, BF),
            sems(4),
            sems(8),
            sems(8),
        ],
    )(land.reshape(landing), *held, w_mix)
    out = (XDIM, SECTORS, TILES, 16, TILE)
    back = call(
        merge_kernel,
        jax.ShapeDtypeStruct(out, BF),
        8,
        [HBM, VMEM],
        HBM,
        [pltpu.VMEM(result, BF), pltpu.VMEM(out, BF), sems(4), sems(8)],
    )(mixed, alpha_land.reshape(landing))
    back, later, beta_late = lax.optimization_barrier((back, coeffs, beta_op[0]))
    home = exchange(back.reshape(256, 16, TILE), ("x", "sym", "z"))
    beta_part = call(
        beta_kernel,
        jax.ShapeDtypeStruct(coeffs.shape, F32),
        12,
        [HBM, HBM],
        HBM,
        [
            pltpu.VMEM(coeffs.shape, BF),
            pltpu.VMEM(beta_late.shape, BF),
            pltpu.VMEM(coeffs.shape, F32),
            sems(2),
            pltpu.SemaphoreType.DMA,
        ],
    )(later, beta_late)
    return call(
        unpack_kernel,
        jax.ShapeDtypeStruct(coeffs.shape, F32),
        12,
        [VMEM, HBM],
        HBM,
        [pltpu.VMEM(coeffs.shape, F32), pltpu.VMEM(coeffs.shape, F32), sems(4), sems(4)],
    )(home.reshape(out), beta_part)


def arrival(block):
    rank = block // ABLK
    return ((rank % XDIM) * TILES + rank // XDIM) * ABLK + block % ABLK


def exchange(array, axes):
    return lax.all_to_all(array, axes, split_axis=0, concat_axis=0, tiled=True)


def solution(mesh):
    fine = Mesh(mesh.devices.reshape(SECTORS, TILES, XDIM), ("sym", "z", "x"))
    rows = ("z", "x")
    in_specs = (
        P(rows, "sym"),
        P("sym", None, None),
        P("sym", None, None, None, None),
        P(),
        P(),
        P(),
        P(),
        P(),
        P(),
        P(),
        P(),
    )
    out_specs = P(rows, "sym")
    return jax.shard_map(
        per_device, mesh=fine, in_specs=in_specs, out_specs=out_specs, check_vma=False
    )
```

```python
import jax
import jax.numpy as jnp
from jax import lax
from jax.experimental import pallas as pl
from jax.experimental.pallas import tpu as pltpu
from jax.sharding import Mesh, PartitionSpec as P

TILE = 128
ABLK = 4
CAP = 2
OPS = 8
SECTORS = 8
RANKS = 32
XDIM = 4
TILES = 8
NBLK = 128
BF = jnp.bfloat16
F32 = jnp.float32
MIB = 1024 * 1024


def interleave(rows, cols):
    r = lax.broadcasted_iota(jnp.int32, (rows, cols), 0)
    k = lax.broadcasted_iota(jnp.int32, (rows, cols), 1)
    return (k == (r % ABLK) * TILE + r // ABLK).astype(F32).astype(BF)


def deinterleave(rows, cols):
    r = lax.broadcasted_iota(jnp.int32, (rows, cols), 0)
    k = lax.broadcasted_iota(jnp.int32, (rows, cols), 1)
    return (r == (k % ABLK) * TILE + k // ABLK).astype(F32).astype(BF)


def pack_kernel(c_hbm, send_hbm, c_ref, t_ref, send_ref, in_sem, out_sem):
    loads = []
    for p in range(ABLK):
        rows = pl.ds(p * TILE, TILE)
        loads.append(pltpu.make_async_copy(c_hbm.at[rows], c_ref.at[rows], in_sem.at[p]))
        loads[-1].start()
    order = interleave(512, 512)
    for p in range(ABLK):
        loads[p].wait()
        for t in range(TILES):
            block = c_ref[p * TILE : (p + 1) * TILE, t * TILE : (t + 1) * TILE]
            t_ref[p * TILE : (p + 1) * TILE, t * TILE : (t + 1) * TILE] = block.T
    stores = []
    for k in range(4):
        both = t_ref[:, k * 2 * TILE : (k + 1) * 2 * TILE]
        moved = jnp.dot(order, both, preferred_element_type=F32).astype(BF)
        for o in range(2):
            part = moved[:, o * TILE : (o + 1) * TILE]
            send_ref[:, 2 * k + o] = part.reshape(XDIM, TILE, TILE)
        here = pl.ds(2 * k, 2)
        stores.append(
            pltpu.make_async_copy(send_ref.at[:, here], send_hbm.at[:, here], out_sem.at[k])
        )
        stores[-1].start()
    for copy in stores:
        copy.wait()


def pick_kernel(op_hbm, out_hbm, op_ref, in_sem, out_sem):
    tile = lax.axis_index("z")
    load = pltpu.make_async_copy(op_hbm.at[0, :, tile], op_ref, in_sem)
    load.start()
    load.wait()
    store = pltpu.make_async_copy(op_ref, out_hbm, out_sem)
    store.start()
    store.wait()


def swap_halves(first, second):
    low = lax.broadcasted_iota(jnp.int32, first.shape, 1) < 4
    lo = jnp.where(low, first, pltpu.roll(second, 4, 1))
    hi = jnp.where(low, pltpu.roll(first, 4, 1), second)
    return lo, hi


def blocks_of(recv_ref, c):
    got = recv_ref[:, c].astype(F32).reshape(16, 2, 2, 8, TILE)
    blocks = []
    for h in range(2):
        blocks += [b.reshape(TILE, TILE) for b in swap_halves(got[:, 0, h], got[:, 1, h])]
    return blocks


def regroup(blocks, out_ref, c):
    sides = []
    for h in range(2):
        first = blocks[2 * h].reshape(16, 8, TILE)
        second = blocks[2 * h + 1].reshape(16, 8, TILE)
        sides.append(swap_halves(first, second))
    for o in range(2):
        both = jnp.concatenate([sides[0][o][:, None], sides[1][o][:, None]], axis=1)
        out_ref[:, o, c] = both.reshape(16, 16, TILE).astype(BF)


def turn_kernel(recv_ref, out_hbm, out_ref, out_sem):
    stores = []
    for c in range(TILES):
        regroup([b.T for b in blocks_of(recv_ref, c)], out_ref, c)
        stores.append(
            pltpu.make_async_copy(out_ref.at[:, :, c], out_hbm.at[:, :, c], out_sem.at[c])
        )
        stores[-1].start()
    for copy in stores:
        copy.wait()


def stacked(w_ref):
    return jnp.concatenate([w_ref[:, g * TILE : (g + 1) * TILE] for g in range(OPS)], axis=0)


def combine(weights, x_ref, c_ref, flip):
    @pl.loop(0, SECTORS // 2)
    def _(half):
        s = half * 2
        for a in range(ABLK):
            pair = jnp.concatenate([x_ref[s, a], x_ref[s + 1, a]], axis=1)
            combo = jnp.dot(weights, pair, preferred_element_type=F32).astype(BF)
            for g in range(OPS):
                rows = combo[g * TILE : (g + 1) * TILE]
                for o in range(2):
                    dest = (s + o) ^ g if flip else s + o
                    c_ref[dest, a * TILE : (a + 1) * TILE, g * TILE : (g + 1) * TILE] = rows[
                        :, o * TILE : (o + 1) * TILE
                    ]


def alpha_kernel(recv_ref, pair_ref, w_ref, out_ref, x_ref, c_ref):
    @pl.loop(0, SECTORS)
    def _(c):
        for a, block in enumerate(blocks_of(recv_ref, c)):
            x_ref[c, a] = block.astype(BF)

    combine(stacked(w_ref), x_ref, c_ref, False)

    @pl.loop(0, SECTORS)
    def _(c):
        res = jnp.dot(c_ref[c], pair_ref[...], preferred_element_type=F32)
        regroup([res[a * TILE : (a + 1) * TILE].T for a in range(ABLK)], out_ref, c)


def landed(land_ref, s, order):
    both = jnp.concatenate([land_ref[:, s + o].reshape(512, TILE) for o in range(2)], axis=1)
    return jnp.dot(order, both, preferred_element_type=F32)


def mixed_kernel(
    land_hbm, o0, o1, o2, o3, o4, o5, o6, o7, w_ref, res_hbm,
    land_ref, x_ref, c_ref, mix_ref, res_ref, land_sem, op_sem, out_sem,
):
    sector = lax.axis_index("sym")
    lands, loads = [], []
    for half in range(SECTORS // 2):
        here = pl.ds(2 * half, 2)
        lands.append(
            pltpu.make_async_copy(land_hbm.at[:, here], land_ref.at[:, here], land_sem.at[half])
        )
        lands[-1].start()
    for k, op_hbm in enumerate((o0, o1, o2, o3, o4, o5, o6, o7)):
        loads.append(pltpu.make_async_copy(op_hbm, mix_ref.at[k], op_sem.at[k]))
        loads[-1].start()
    order = deinterleave(512, 512)
    for half in range(SECTORS // 2):
        lands[half].wait()
        moved = landed(land_ref, 2 * half, order)
        for a in range(ABLK):
            for o in range(2):
                block = moved[a * TILE : (a + 1) * TILE, o * TILE : (o + 1) * TILE]
                x_ref[2 * half + o, a] = block.T.astype(BF)

    combine(stacked(w_ref), x_ref, c_ref, True)
    for copy in loads:
        copy.wait()

    @pl.loop(0, SECTORS)
    def _(d):
        ops = jnp.concatenate([mix_ref[sector ^ d ^ g, g] for g in range(OPS)], axis=0)
        res_ref[d] = jnp.dot(c_ref[d], ops, preferred_element_type=F32).astype(BF)
        pltpu.make_async_copy(res_ref.at[d], res_hbm.at[d], out_sem.at[d]).start()

    @pl.loop(0, SECTORS)
    def _(d):
        pltpu.make_async_copy(res_ref.at[d], res_hbm.at[d], out_sem.at[d]).wait()


def merge_kernel(res_hbm, land_ref, out_hbm, res_ref, out_ref, in_sem, out_sem):
    loads = []
    for half in range(SECTORS // 2):
        here = pl.ds(2 * half, 2)
        loads.append(
            pltpu.make_async_copy(res_hbm.at[here], res_ref.at[here], in_sem.at[half])
        )
        loads[-1].start()
    order = deinterleave(512, 512)
    stores = []
    for half in range(SECTORS // 2):
        moved = landed(land_ref, 2 * half, order).astype(BF)
        loads[half].wait()
        for o in range(2):
            d = 2 * half + o
            blocks = []
            for a in range(ABLK):
                rows = slice(a * TILE, (a + 1) * TILE)
                blocks.append(res_ref[d, rows].astype(F32) + moved[rows, o * TILE : (o + 1) * TILE].T.astype(F32))
            sides = []
            for h in range(2):
                first = blocks[2 * h].reshape(16, 8, TILE)
                second = blocks[2 * h + 1].reshape(16, 8, TILE)
                sides.append(swap_halves(first, second))
            for side in range(2):
                both = jnp.concatenate([sides[0][side][:, None], sides[1][side][:, None]], axis=1)
                both = both.reshape(TILES, 2, 16, TILE).astype(BF)
                for v in range(2):
                    out_ref[2 * v + side, d] = both[:, v]
            stores.append(
                pltpu.make_async_copy(out_ref.at[:, d], out_hbm.at[:, d], out_sem.at[d])
            )
            stores[-1].start()
    for copy in stores:
        copy.wait()


def beta_kernel(c_hbm, op_hbm, out_hbm, c_ref, op_ref, out_ref, in_sem, out_sem):
    loads = [
        pltpu.make_async_copy(c_hbm, c_ref, in_sem.at[0]),
        pltpu.make_async_copy(op_hbm, op_ref, in_sem.at[1]),
    ]
    for copy in loads:
        copy.start()
    for copy in loads:
        copy.wait()
    for k in range(4):
        cols = slice(k * 2 * TILE, (k + 1) * 2 * TILE)
        out_ref[:, cols] = jnp.dot(
            c_ref[...], op_ref[:, cols], preferred_element_type=F32
        ).astype(BF)
    store = pltpu.make_async_copy(out_ref, out_hbm, out_sem)
    store.start()
    store.wait()


def unpack_kernel(recv_ref, beta_hbm, out_hbm, beta_ref, out_ref, in_sem, out_sem):
    loads = []
    for k in range(4):
        cols = pl.ds(k * 2 * TILE, 2 * TILE)
        loads.append(
            pltpu.make_async_copy(beta_hbm.at[:, cols], beta_ref.at[:, cols], in_sem.at[k])
        )
        loads[-1].start()
    order = deinterleave(512, 512)
    stores = []
    for k in range(4):
        both = jnp.concatenate(
            [recv_ref[:, :, u].reshape(512, TILE) for u in (2 * k, 2 * k + 1)], axis=1
        )
        moved = jnp.dot(order, both, preferred_element_type=F32)
        loads[k].wait()
        cols = pl.ds(k * 2 * TILE, 2 * TILE)
        out_ref[:, cols] = beta_ref[:, cols].astype(F32) + moved
        stores.append(
            pltpu.make_async_copy(out_ref.at[:, cols], out_hbm.at[:, cols], out_sem.at[k])
        )
        stores[-1].start()
    for copy in stores:
        copy.wait()


HBM, VMEM = pltpu.HBM, pltpu.VMEM


def call(kernel, out_shape, mib, ins, out, scratch):
    if out is HBM:
        out_shape = HBM(out_shape.shape, out_shape.dtype)
    run = pl.pallas_call(
        kernel,
        out_shape=out_shape,
        in_specs=[pl.BlockSpec(memory_space=place) for place in ins],
        out_specs=pl.BlockSpec(memory_space=out),
        scratch_shapes=scratch,
        compiler_params=pltpu.CompilerParams(vmem_limit_bytes=mib * MIB),
    )

    def placed(*args):
        return run(
            *(
                pltpu.with_memory_space_constraint(x, HBM) if place is HBM else x
                for x, place in zip(args, ins)
            )
        )

    return placed


def sems(count):
    return pltpu.SemaphoreType.DMA((count,))


def signed_weights(source, sign, pair):
    key = pair * NBLK + source
    ids = jnp.arange(OPS * NBLK, dtype=jnp.int32)
    hit = key[:, :, None] == ids[None, None, :]
    factor = (1 - 2 * sign).astype(F32)
    return jnp.sum(jnp.where(hit, factor[:, :, None], 0.0), axis=1).astype(BF)


def swapped(array, mask):
    return lax.ppermute(array, "sym", [(s, s ^ mask) for s in range(SECTORS)])


def per_device(
    coeffs,
    beta_op,
    mix_op,
    pair_op,
    send_list,
    mix_slot,
    mix_sign,
    mix_pair,
    aa_src,
    aa_sign,
    aa_pair,
):
    sent = (XDIM, TILES, TILE, TILE)
    send = call(
        pack_kernel,
        jax.ShapeDtypeStruct(sent, BF),
        8,
        [HBM],
        HBM,
        [pltpu.VMEM((512, 1024), BF)] * 2 + [pltpu.VMEM(sent, BF), sems(4), sems(4)],
    )(coeffs)
    send, picked = lax.optimization_barrier((send, mix_op))
    mine = call(
        pick_kernel,
        jax.ShapeDtypeStruct((OPS, TILE, TILE), BF),
        4,
        [HBM],
        HBM,
        [pltpu.VMEM((OPS, TILE, TILE), BF), pltpu.SemaphoreType.DMA, pltpu.SemaphoreType.DMA],
    )(picked)
    ops = {0: mine}
    for k in (2, 4, 6, 1):
        ops[k] = swapped(mine, k)
    recv = exchange(send.reshape(32, TILE, TILE), ("x", "z"))

    table = jnp.transpose(send_list, (1, 0, 2)).reshape(RANKS, RANKS * CAP)
    slots = jnp.arange(RANKS * CAP, dtype=jnp.int32)
    table = jnp.broadcast_to(table[:, None, :], (RANKS, ABLK, RANKS * CAP)).reshape(NBLK, 1, RANKS * CAP)
    owned = jnp.sum(jnp.where(mix_slot[:, :, None] == slots[None, None, :], table, 0), axis=2)
    source = (mix_slot // CAP) * ABLK + owned
    w_mix = signed_weights(arrival(source), mix_sign, mix_pair)
    w_alpha = signed_weights(arrival(aa_src), aa_sign, aa_pair)
    pairs = jnp.transpose(pair_op, (0, 2, 1)).reshape(OPS * TILE, TILE)
    ops[2], ops[4], ops[6], w_mix, w_alpha, pairs = lax.optimization_barrier(
        (ops[2], ops[4], ops[6], w_mix, w_alpha, pairs)
    )
    for k in (2, 4, 6):
        ops[k + 1] = swapped(ops[k], 1)
    held = [ops[k] for k in range(SECTORS)]
    recv, held, w_mix, w_alpha, pairs = lax.optimization_barrier(
        (recv, held, w_mix, w_alpha, pairs)
    )
    recv = recv.reshape(RANKS, TILES, 16, TILE)
    parted = (16, 2, TILES, 16, TILE)
    grouped = jax.ShapeDtypeStruct(parted, BF)
    turned = call(turn_kernel, grouped, 6, [VMEM], HBM, [pltpu.VMEM(parted, BF), sems(8)])(recv)
    land = exchange(turned.reshape(32, TILE, TILE), ("x", "sym"))

    blocks = pltpu.VMEM((SECTORS, ABLK, TILE, TILE), BF)
    combos = pltpu.VMEM((SECTORS, 4 * TILE, OPS * TILE), BF)
    alpha = call(alpha_kernel, grouped, 18, [VMEM] * 3, VMEM, [blocks, combos])(
        recv, pairs, w_alpha
    )
    alpha_land = exchange(alpha.reshape(32, TILE, TILE), ("x", "sym"))
    landing = (XDIM, SECTORS, TILE, TILE)
    result = (SECTORS, 512, TILE)
    mixed = call(
        mixed_kernel,
        jax.ShapeDtypeStruct(result, BF),
        24,
        [HBM] * 9 + [VMEM],
        HBM,
        [
            pltpu.VMEM(landing, BF),
            blocks,
            combos,
            pltpu.VMEM((SECTORS, OPS, TILE, TILE), BF),
            pltpu.VMEM(result, BF),
            sems(4),
            sems(8),
            sems(8),
        ],
    )(land.reshape(landing), *held, w_mix)
    out = (XDIM, SECTORS, TILES, 16, TILE)
    back = call(
        merge_kernel,
        jax.ShapeDtypeStruct(out, BF),
        8,
        [HBM, VMEM],
        HBM,
        [pltpu.VMEM(result, BF), pltpu.VMEM(out, BF), sems(4), sems(8)],
    )(mixed, alpha_land.reshape(landing))
    back, later, beta_late = lax.optimization_barrier((back, coeffs, beta_op[0]))
    home = exchange(back.reshape(256, 16, TILE), ("x", "sym", "z"))
    beta_part = call(
        beta_kernel,
        jax.ShapeDtypeStruct(coeffs.shape, BF),
        12,
        [HBM, HBM],
        HBM,
        [
            pltpu.VMEM(coeffs.shape, BF),
            pltpu.VMEM(beta_late.shape, BF),
            pltpu.VMEM(coeffs.shape, BF),
            sems(2),
            pltpu.SemaphoreType.DMA,
        ],
    )(later, beta_late)
    return call(
        unpack_kernel,
        jax.ShapeDtypeStruct(coeffs.shape, F32),
        12,
        [VMEM, HBM],
        HBM,
        [pltpu.VMEM(coeffs.shape, BF), pltpu.VMEM(coeffs.shape, F32), sems(4), sems(4)],
    )(home.reshape(out), beta_part)


def arrival(block):
    rank = block // ABLK
    return ((rank % XDIM) * TILES + rank // XDIM) * ABLK + block % ABLK


def exchange(array, axes):
    return lax.all_to_all(array, axes, split_axis=0, concat_axis=0, tiled=True)


def solution(mesh):
    fine = Mesh(mesh.devices.reshape(SECTORS, TILES, XDIM), ("sym", "z", "x"))
    rows = ("z", "x")
    in_specs = (
        P(rows, "sym"),
        P("sym", None, None),
        P("sym", None, None, None, None),
        P(),
        P(),
        P(),
        P(),
        P(),
        P(),
        P(),
        P(),
    )
    out_specs = P(rows, "sym")
    return jax.shard_map(
        per_device, mesh=fine, in_specs=in_specs, out_specs=out_specs, check_vma=False
    )
```

```python
import jax
import jax.numpy as jnp
from jax import lax
from jax.experimental import pallas as pl
from jax.experimental.pallas import tpu as pltpu
from jax.sharding import Mesh, PartitionSpec as P

TILE = 128
ABLK = 4
CAP = 2
OPS = 8
SECTORS = 8
RANKS = 32
XDIM = 4
TILES = 8
NBLK = 128
BF = jnp.bfloat16
F32 = jnp.float32
MIB = 1024 * 1024


def interleave(rows, cols):
    r = lax.broadcasted_iota(jnp.int32, (rows, cols), 0)
    k = lax.broadcasted_iota(jnp.int32, (rows, cols), 1)
    return (k == (r % ABLK) * TILE + r // ABLK).astype(F32).astype(BF)


def deinterleave(rows, cols):
    r = lax.broadcasted_iota(jnp.int32, (rows, cols), 0)
    k = lax.broadcasted_iota(jnp.int32, (rows, cols), 1)
    return (r == (k % ABLK) * TILE + k // ABLK).astype(F32).astype(BF)


def pack_kernel(c_hbm, send_hbm, c_ref, t_ref, send_ref, in_sem, out_sem):
    loads = []
    for p in range(ABLK):
        rows = pl.ds(p * TILE, TILE)
        loads.append(pltpu.make_async_copy(c_hbm.at[rows], c_ref.at[rows], in_sem.at[p]))
        loads[-1].start()
    order = interleave(512, 512)
    for p in range(ABLK):
        loads[p].wait()
        for t in range(TILES):
            block = c_ref[p * TILE : (p + 1) * TILE, t * TILE : (t + 1) * TILE]
            t_ref[p * TILE : (p + 1) * TILE, t * TILE : (t + 1) * TILE] = block.T
    stores = []
    for k in range(4):
        both = t_ref[:, k * 2 * TILE : (k + 1) * 2 * TILE]
        moved = jnp.dot(order, both, preferred_element_type=F32).astype(BF)
        for o in range(2):
            part = moved[:, o * TILE : (o + 1) * TILE]
            u = 2 * k + o
            send_ref[:, u] = part.reshape(XDIM, TILE, TILE)
            stores.append(
                pltpu.make_async_copy(send_ref.at[:, u], send_hbm.at[:, u], out_sem.at[u])
            )
            stores[-1].start()
    for copy in stores:
        copy.wait()


def pick_kernel(op_hbm, out_hbm, op_ref, in_sem, out_sem):
    tile = lax.axis_index("z")
    load = pltpu.make_async_copy(op_hbm.at[0, :, tile], op_ref, in_sem)
    load.start()
    load.wait()
    store = pltpu.make_async_copy(op_ref, out_hbm, out_sem)
    store.start()
    store.wait()


def swap_halves(first, second):
    low = lax.broadcasted_iota(jnp.int32, first.shape, 1) < 4
    lo = jnp.where(low, first, pltpu.roll(second, 4, 1))
    hi = jnp.where(low, pltpu.roll(first, 4, 1), second)
    return lo, hi


def blocks_of(recv_ref, c):
    got = recv_ref[:, c].astype(F32).reshape(16, 2, 2, 8, TILE)
    blocks = []
    for h in range(2):
        blocks += [b.reshape(TILE, TILE) for b in swap_halves(got[:, 0, h], got[:, 1, h])]
    return blocks


def regroup(blocks, out_ref, c):
    sides = []
    for h in range(2):
        first = blocks[2 * h].reshape(16, 8, TILE)
        second = blocks[2 * h + 1].reshape(16, 8, TILE)
        sides.append(swap_halves(first, second))
    for o in range(2):
        both = jnp.concatenate([sides[0][o][:, None], sides[1][o][:, None]], axis=1)
        out_ref[:, o, c] = both.reshape(16, 16, TILE).astype(BF)


def turn_kernel(recv_ref, out_hbm, out_ref, out_sem):
    stores = []
    for c in range(TILES):
        regroup([b.T for b in blocks_of(recv_ref, c)], out_ref, c)
        stores.append(
            pltpu.make_async_copy(out_ref.at[:, :, c], out_hbm.at[:, :, c], out_sem.at[c])
        )
        stores[-1].start()
    for copy in stores:
        copy.wait()


def stacked(w_ref):
    return jnp.concatenate([w_ref[:, g * TILE : (g + 1) * TILE] for g in range(OPS)], axis=0)


def combine(weights, x_ref, c_ref, flip):
    @pl.loop(0, SECTORS // 2)
    def _(half):
        s = half * 2
        for a in range(ABLK):
            pair = jnp.concatenate([x_ref[s, a], x_ref[s + 1, a]], axis=1)
            combo = jnp.dot(weights, pair, preferred_element_type=F32).astype(BF)
            for g in range(OPS):
                rows = combo[g * TILE : (g + 1) * TILE]
                for o in range(2):
                    dest = (s + o) ^ g if flip else s + o
                    c_ref[dest, a * TILE : (a + 1) * TILE, g * TILE : (g + 1) * TILE] = rows[
                        :, o * TILE : (o + 1) * TILE
                    ]


def alpha_kernel(recv_ref, pair_ref, w_ref, out_ref, x_ref, c_ref):
    @pl.loop(0, SECTORS)
    def _(c):
        for a, block in enumerate(blocks_of(recv_ref, c)):
            x_ref[c, a] = block.astype(BF)

    combine(stacked(w_ref), x_ref, c_ref, False)

    @pl.loop(0, SECTORS)
    def _(c):
        res = jnp.dot(c_ref[c], pair_ref[...], preferred_element_type=F32)
        regroup([res[a * TILE : (a + 1) * TILE].T for a in range(ABLK)], out_ref, c)


def landed(land_ref, s, order):
    both = jnp.concatenate([land_ref[:, s + o].reshape(512, TILE) for o in range(2)], axis=1)
    return jnp.dot(order, both, preferred_element_type=F32)


def mixed_kernel(
    land_hbm, o0, o1, o2, o3, o4, o5, o6, o7, w_ref, res_hbm,
    land_ref, x_ref, c_ref, mix_ref, res_ref, land_sem, op_sem, out_sem,
):
    sector = lax.axis_index("sym")
    lands, loads = [], []
    for half in range(SECTORS // 2):
        here = pl.ds(2 * half, 2)
        lands.append(
            pltpu.make_async_copy(land_hbm.at[:, here], land_ref.at[:, here], land_sem.at[half])
        )
        lands[-1].start()
    for k, op_hbm in enumerate((o0, o1, o2, o3, o4, o5, o6, o7)):
        loads.append(pltpu.make_async_copy(op_hbm, mix_ref.at[k], op_sem.at[k]))
        loads[-1].start()
    order = deinterleave(512, 512)
    for half in range(SECTORS // 2):
        lands[half].wait()
        moved = landed(land_ref, 2 * half, order)
        for a in range(ABLK):
            for o in range(2):
                block = moved[a * TILE : (a + 1) * TILE, o * TILE : (o + 1) * TILE]
                x_ref[2 * half + o, a] = block.T.astype(BF)

    combine(stacked(w_ref), x_ref, c_ref, True)
    for copy in loads:
        copy.wait()

    @pl.loop(0, SECTORS)
    def _(d):
        ops = jnp.concatenate([mix_ref[sector ^ d ^ g, g] for g in range(OPS)], axis=0)
        res_ref[d] = jnp.dot(c_ref[d], ops, preferred_element_type=F32).astype(BF)
        pltpu.make_async_copy(res_ref.at[d], res_hbm.at[d], out_sem.at[d]).start()

    @pl.loop(0, SECTORS)
    def _(d):
        pltpu.make_async_copy(res_ref.at[d], res_hbm.at[d], out_sem.at[d]).wait()


def merge_kernel(res_hbm, land_ref, out_hbm, res_ref, out_ref, in_sem, out_sem):
    loads = []
    for half in range(SECTORS // 2):
        here = pl.ds(2 * half, 2)
        loads.append(
            pltpu.make_async_copy(res_hbm.at[here], res_ref.at[here], in_sem.at[half])
        )
        loads[-1].start()
    order = deinterleave(512, 512)
    stores = []
    for half in range(SECTORS // 2):
        moved = landed(land_ref, 2 * half, order).astype(BF)
        loads[half].wait()
        for o in range(2):
            d = 2 * half + o
            blocks = []
            for a in range(ABLK):
                rows = slice(a * TILE, (a + 1) * TILE)
                blocks.append(res_ref[d, rows].astype(F32) + moved[rows, o * TILE : (o + 1) * TILE].T.astype(F32))
            sides = []
            for h in range(2):
                first = blocks[2 * h].reshape(16, 8, TILE)
                second = blocks[2 * h + 1].reshape(16, 8, TILE)
                sides.append(swap_halves(first, second))
            for side in range(2):
                both = jnp.concatenate([sides[0][side][:, None], sides[1][side][:, None]], axis=1)
                both = both.reshape(TILES, 2, 16, TILE).astype(BF)
                for v in range(2):
                    out_ref[2 * v + side, d] = both[:, v]
            stores.append(
                pltpu.make_async_copy(out_ref.at[:, d], out_hbm.at[:, d], out_sem.at[d])
            )
            stores[-1].start()
    for copy in stores:
        copy.wait()


def beta_kernel(c_hbm, op_hbm, out_hbm, c_ref, op_ref, out_ref, in_sem, out_sem):
    loads = [
        pltpu.make_async_copy(c_hbm, c_ref, in_sem.at[0]),
        pltpu.make_async_copy(op_hbm, op_ref, in_sem.at[1]),
    ]
    for copy in loads:
        copy.start()
    for copy in loads:
        copy.wait()
    for k in range(4):
        cols = slice(k * 2 * TILE, (k + 1) * 2 * TILE)
        out_ref[:, cols] = jnp.dot(
            c_ref[...], op_ref[:, cols], preferred_element_type=F32
        ).astype(BF)
    store = pltpu.make_async_copy(out_ref, out_hbm, out_sem)
    store.start()
    store.wait()


def unpack_kernel(recv_ref, beta_hbm, out_hbm, beta_ref, out_ref, in_sem, out_sem):
    loads = []
    for k in range(4):
        cols = pl.ds(k * 2 * TILE, 2 * TILE)
        loads.append(
            pltpu.make_async_copy(beta_hbm.at[:, cols], beta_ref.at[:, cols], in_sem.at[k])
        )
        loads[-1].start()
    order = deinterleave(512, 512)
    stores = []
    for k in range(4):
        both = jnp.concatenate(
            [recv_ref[:, :, u].reshape(512, TILE) for u in (2 * k, 2 * k + 1)], axis=1
        )
        moved = jnp.dot(order, both, preferred_element_type=F32)
        loads[k].wait()
        cols = pl.ds(k * 2 * TILE, 2 * TILE)
        out_ref[:, cols] = beta_ref[:, cols].astype(F32) + moved
        stores.append(
            pltpu.make_async_copy(out_ref.at[:, cols], out_hbm.at[:, cols], out_sem.at[k])
        )
        stores[-1].start()
    for copy in stores:
        copy.wait()


HBM, VMEM = pltpu.HBM, pltpu.VMEM


def call(kernel, out_shape, mib, ins, out, scratch):
    if out is HBM:
        out_shape = HBM(out_shape.shape, out_shape.dtype)
    run = pl.pallas_call(
        kernel,
        out_shape=out_shape,
        in_specs=[pl.BlockSpec(memory_space=place) for place in ins],
        out_specs=pl.BlockSpec(memory_space=out),
        scratch_shapes=scratch,
        compiler_params=pltpu.CompilerParams(vmem_limit_bytes=mib * MIB),
    )

    def placed(*args):
        return run(
            *(
                pltpu.with_memory_space_constraint(x, HBM) if place is HBM else x
                for x, place in zip(args, ins)
            )
        )

    return placed


def sems(count):
    return pltpu.SemaphoreType.DMA((count,))


def signed_weights(source, sign, pair):
    key = pair * NBLK + source
    ids = jnp.arange(OPS * NBLK, dtype=jnp.int32)
    hit = key[:, :, None] == ids[None, None, :]
    factor = (1 - 2 * sign).astype(F32)
    return jnp.sum(jnp.where(hit, factor[:, :, None], 0.0), axis=1).astype(BF)


def swapped(array, mask):
    return lax.ppermute(array, "sym", [(s, s ^ mask) for s in range(SECTORS)])


def per_device(
    coeffs,
    beta_op,
    mix_op,
    pair_op,
    send_list,
    mix_slot,
    mix_sign,
    mix_pair,
    aa_src,
    aa_sign,
    aa_pair,
):
    sent = (XDIM, TILES, TILE, TILE)
    send = call(
        pack_kernel,
        jax.ShapeDtypeStruct(sent, BF),
        8,
        [HBM],
        HBM,
        [pltpu.VMEM((512, 1024), BF)] * 2 + [pltpu.VMEM(sent, BF), sems(4), sems(8)],
    )(coeffs)
    send, picked = lax.optimization_barrier((send, mix_op))
    mine = call(
        pick_kernel,
        jax.ShapeDtypeStruct((OPS, TILE, TILE), BF),
        4,
        [HBM],
        HBM,
        [pltpu.VMEM((OPS, TILE, TILE), BF), pltpu.SemaphoreType.DMA, pltpu.SemaphoreType.DMA],
    )(picked)
    ops = {0: mine}
    for k in (2, 4, 6, 1):
        ops[k] = swapped(mine, k)
    recv = exchange(send.reshape(32, TILE, TILE), ("x", "z"))

    table = jnp.transpose(send_list, (1, 0, 2)).reshape(RANKS, RANKS * CAP)
    slots = jnp.arange(RANKS * CAP, dtype=jnp.int32)
    table = jnp.broadcast_to(table[:, None, :], (RANKS, ABLK, RANKS * CAP)).reshape(NBLK, 1, RANKS * CAP)
    owned = jnp.sum(jnp.where(mix_slot[:, :, None] == slots[None, None, :], table, 0), axis=2)
    source = (mix_slot // CAP) * ABLK + owned
    w_mix = signed_weights(arrival(source), mix_sign, mix_pair)
    w_alpha = signed_weights(arrival(aa_src), aa_sign, aa_pair)
    pairs = jnp.transpose(pair_op, (0, 2, 1)).reshape(OPS * TILE, TILE)
    ops[2], ops[4], ops[6], w_mix, w_alpha, pairs = lax.optimization_barrier(
        (ops[2], ops[4], ops[6], w_mix, w_alpha, pairs)
    )
    for k in (2, 4, 6):
        ops[k + 1] = swapped(ops[k], 1)
    held = [ops[k] for k in range(SECTORS)]
    recv, held, w_mix, w_alpha, pairs = lax.optimization_barrier(
        (recv, held, w_mix, w_alpha, pairs)
    )
    recv = recv.reshape(RANKS, TILES, 16, TILE)
    parted = (16, 2, TILES, 16, TILE)
    grouped = jax.ShapeDtypeStruct(parted, BF)
    turned = call(turn_kernel, grouped, 6, [VMEM], HBM, [pltpu.VMEM(parted, BF), sems(8)])(recv)
    land = exchange(turned.reshape(32, TILE, TILE), ("x", "sym"))

    blocks = pltpu.VMEM((SECTORS, ABLK, TILE, TILE), BF)
    combos = pltpu.VMEM((SECTORS, 4 * TILE, OPS * TILE), BF)
    alpha = call(alpha_kernel, grouped, 18, [VMEM] * 3, VMEM, [blocks, combos])(
        recv, pairs, w_alpha
    )
    alpha_land = exchange(alpha.reshape(32, TILE, TILE), ("x", "sym"))
    landing = (XDIM, SECTORS, TILE, TILE)
    result = (SECTORS, 512, TILE)
    mixed = call(
        mixed_kernel,
        jax.ShapeDtypeStruct(result, BF),
        24,
        [HBM] * 9 + [VMEM],
        HBM,
        [
            pltpu.VMEM(landing, BF),
            blocks,
            combos,
            pltpu.VMEM((SECTORS, OPS, TILE, TILE), BF),
            pltpu.VMEM(result, BF),
            sems(4),
            sems(8),
            sems(8),
        ],
    )(land.reshape(landing), *held, w_mix)
    out = (XDIM, SECTORS, TILES, 16, TILE)
    back = call(
        merge_kernel,
        jax.ShapeDtypeStruct(out, BF),
        8,
        [HBM, VMEM],
        HBM,
        [pltpu.VMEM(result, BF), pltpu.VMEM(out, BF), sems(4), sems(8)],
    )(mixed, alpha_land.reshape(landing))
    back, later, beta_late = lax.optimization_barrier((back, coeffs, beta_op[0]))
    home = exchange(back.reshape(256, 16, TILE), ("x", "sym", "z"))
    beta_part = call(
        beta_kernel,
        jax.ShapeDtypeStruct(coeffs.shape, BF),
        12,
        [HBM, HBM],
        HBM,
        [
            pltpu.VMEM(coeffs.shape, BF),
            pltpu.VMEM(beta_late.shape, BF),
            pltpu.VMEM(coeffs.shape, BF),
            sems(2),
            pltpu.SemaphoreType.DMA,
        ],
    )(later, beta_late)
    return call(
        unpack_kernel,
        jax.ShapeDtypeStruct(coeffs.shape, F32),
        12,
        [VMEM, HBM],
        HBM,
        [pltpu.VMEM(coeffs.shape, BF), pltpu.VMEM(coeffs.shape, F32), sems(4), sems(4)],
    )(home.reshape(out), beta_part)


def arrival(block):
    rank = block // ABLK
    return ((rank % XDIM) * TILES + rank // XDIM) * ABLK + block % ABLK


def exchange(array, axes):
    return lax.all_to_all(array, axes, split_axis=0, concat_axis=0, tiled=True)


def solution(mesh):
    fine = Mesh(mesh.devices.reshape(SECTORS, TILES, XDIM), ("sym", "z", "x"))
    rows = ("z", "x")
    in_specs = (
        P(rows, "sym"),
        P("sym", None, None),
        P("sym", None, None, None, None),
        P(),
        P(),
        P(),
        P(),
        P(),
        P(),
        P(),
        P(),
    )
    out_specs = P(rows, "sym")
    return jax.shard_map(
        per_device, mesh=fine, in_specs=in_specs, out_specs=out_specs, check_vma=False
    )
```
